32 devices in a mesh: dp: 8 (over z, y), mp: 4 (over x, core).
Axes of the slice: x: 2, y: 2, z: 4, core: 2. Of those that a mesh axis runs over, the one named last changes fastest.
Arguments:
- tokens: bfloat16 [8192, 2048], P('dp'), may hold values from -6 to 6
- cotangent: bfloat16 [8192, 2048], P('dp'), may hold values from -6 to 6
- query_weight: bfloat16 [2048, 2048], P('dp', 'mp'), may hold values from -0.125 to 0.125
- key_matrix: bfloat16 [2048, 1024], P('dp', 'mp'), may hold values from -0.125 to 0.125
- value_matrix: bfloat16 [2048, 1024], P('dp', 'mp'), may hold values from -0.125 to 0.125
- head_gate_weight: bfloat16 [2048, 16], P('dp', 'mp'), may hold values from -0.125 to 0.125
- out_weight: bfloat16 [2048, 2048], P('mp', 'dp'), may hold values from -3 to 3
- gate_weight: bfloat16 [2048, 6144], P('dp', 'mp'), may hold values from -0.125 to 0.125
- up_weight: bfloat16 [2048, 6144], P('dp', 'mp'), may hold values from -0.125 to 0.125
- down_weight: bfloat16 [6144, 2048], P('mp', 'dp'), may hold values from -0.078125 to 0.078125
- norm_attn: bfloat16 [2048], P('dp'), may hold values from 0.5 to 1.5
- norm_mlp: bfloat16 [2048], P('dp'), may hold values from 0.5 to 1.5
- norm_query: bfloat16 [128], replicated, may hold values from 0.25 to 1.75
- norm_key: bfloat16 [128], replicated, may hold values from 0.25 to 1.75
- cont_lengths: int32 [2, 3, 2, 4], replicated, may hold values from 1 to 256, 512 in all within a row
Outputs:
- layer_out: bfloat16 [8192, 2048], P('dp')
- tokens_grad: float32 [8192, 2048], P('dp')
- query_weight_grad: float32 [2048, 2048], P('dp', 'mp')
- key_weight_grad: float32 [2048, 1024], P('dp', 'mp')
- value_weight_grad: float32 [2048, 1024], P('dp', 'mp')
- head_gate_weight_grad: float32 [2048, 16], P('dp', 'mp')
- out_weight_grad: float32 [2048, 2048], P('mp', 'dp')
- gate_weight_grad: float32 [2048, 6144], P('dp', 'mp')
- up_weight_grad: float32 [2048, 6144], P('dp', 'mp')
- down_weight_grad: float32 [6144, 2048], P('mp', 'dp')
- norm_attn_grad: float32 [2048], P('dp')
- norm_mlp_grad: float32 [2048], P('dp')
- norm_query_grad: float32 [128], replicated
- norm_key_grad: float32 [128], replicated
The draws below stay inside these ranges and needn't reach their ends.
Inputs may be any that keep to these rules, and one draw needn't show every extreme that they name: `cont_lengths`: each row holds the lengths of the 4 continuations of one device in one micro-batch, in order; a row sums to 512 and its longest length is exactly 256.
All inputs are finite; a program needn't handle non-finite values.
Results may differ from the reference program's by a relative error of at most 0.024.
Values may be sent and summed in bfloat16 or wider, within the bound.
No kernel may reach another device: no remote copies, remote signals or barrier semaphores. Data moves between devices by JAX's collectives and lax.ppermute only.
A program may use at most 256 MiB of HBM per device.

```python
import math
import jax
import jax.numpy as jnp
import numpy as np
from jax import lax

MODEL_WIDTH = 2048
QUERY_HEADS = 16
KEY_HEADS = 8
HEAD_SIZE = 128
FF = 6144
PROMPT_TOKENS = 512
MICRO_BATCHES = 2
GROUP_DEVICES = 4
CONT_MAX = 256
NCONT = 4
PROMPT_GROUPS = 2
TOKEN_COUNT = 8192


def levels(stream_key, extent, cuts, low, largest):
    def one(dim, parts):
        steps = jax.random.uniform(jax.random.fold_in(jax.random.fold_in(stream_key, 6), dim), (parts,), jnp.float32, low / len(cuts), largest / len(cuts))
        return jnp.repeat(jnp.exp(steps), extent[dim] // parts).reshape((-1,) + (1,) * (len(extent) - dim - 1))

    loudness = one(*cuts[0])
    for cut in cuts[1:]:
        loudness = loudness * one(*cut)
    return loudness


def split_up(count, total, reach, slope):
    weights = [(1 << 20) // math.isqrt(rank ** slope) + 1 for rank in range(2, count + 1)]
    spare, counts = total - reach - (count - 1), [1] * (count - 1)
    while spare > 0:
        candidates = [i for i in range(count - 1) if counts[i] < reach]
        whole, left = sum([weights[i] for i in candidates]), spare
        for i in candidates:
            more = min(reach - counts[i], max(1, left * weights[i] // whole), spare)
            counts[i] = counts[i] + more
            spare = spare - more
    return np.array([reach] + counts)


def uneven(key, number_of, total, limit, slope):
    if number_of == 2:
        one = jax.random.randint(key, (), max(1, total - limit), min(limit, total - 1) + 1)
        return jnp.stack([one, total - one])
    sizes = jnp.asarray(split_up(number_of, total, limit, slope), jnp.int32)
    couples = (number_of - 1) // 2
    giver, sink = sizes[1:1 + 2 * couples:2], sizes[2:2 + 2 * couples:2]
    margin = jnp.minimum(giver - 1, limit - sink)
    passed = jax.random.randint(jax.random.fold_in(key, 1), (couples,), 0, 1 << 20) % (margin + 1)
    sizes = sizes.at[1:1 + 2 * couples:2].set(giver - passed).at[2:2 + 2 * couples:2].set(sink + passed)
    return sizes[jax.random.permutation(jax.random.fold_in(key, 2), number_of)]


def gaussian(stream_key, shape, spread, bound, split=(), kind=jnp.bfloat16):
    factor_of = levels(stream_key, shape, split, -0.22, 0.18) if split else 1.0
    entries = jax.random.normal(stream_key, shape, jnp.float32) * spread * factor_of
    return jnp.minimum(jnp.maximum(entries, -bound), bound).astype(kind)


def setup_inputs(seed: int = 0) -> dict:
    splits = jax.random.split(jax.random.key(seed), 16)
    return {
        "tokens": gaussian(splits[0], (TOKEN_COUNT, MODEL_WIDTH), 1.0, 6.0, ((0, 8),)),
        "cotangent": gaussian(splits[1], (TOKEN_COUNT, MODEL_WIDTH), 1.0, 6.0, ((0, 8),)),
        "query_weight": gaussian(splits[2], (MODEL_WIDTH, QUERY_HEADS * HEAD_SIZE), MODEL_WIDTH ** -0.5, 0.125, ((0, 8), (1, 4))),
        "key_matrix": gaussian(splits[3], (MODEL_WIDTH, KEY_HEADS * HEAD_SIZE), MODEL_WIDTH ** -0.5, 0.125, ((0, 8), (1, 4))),
        "value_matrix": gaussian(splits[4], (MODEL_WIDTH, KEY_HEADS * HEAD_SIZE), MODEL_WIDTH ** -0.5, 0.125, ((0, 8), (1, 4))),
        "head_gate_weight": gaussian(splits[5], (MODEL_WIDTH, QUERY_HEADS), MODEL_WIDTH ** -0.5, 0.125, ((0, 8), (1, 4))),
        "out_weight": gaussian(splits[6], (QUERY_HEADS * HEAD_SIZE, MODEL_WIDTH), (QUERY_HEADS * HEAD_SIZE // PROMPT_TOKENS) ** -0.5, 3.0, ((0, 4), (1, 8))),
        "gate_weight": gaussian(splits[7], (MODEL_WIDTH, FF), MODEL_WIDTH ** -0.5, 0.125, ((0, 8), (1, 4))),
        "up_weight": gaussian(splits[8], (MODEL_WIDTH, FF), MODEL_WIDTH ** -0.5, 0.125, ((0, 8), (1, 4))),
        "down_weight": gaussian(splits[9], (FF, MODEL_WIDTH), FF ** -0.5, 0.078125, ((0, 4), (1, 8))),
        "norm_attn": jnp.clip(1.0 + 0.1 * jax.random.normal(splits[10], (MODEL_WIDTH,), jnp.float32), 0.5, 1.5).astype(jnp.bfloat16),
        "norm_mlp": jnp.clip(1.0 + 0.1 * jax.random.normal(splits[11], (MODEL_WIDTH,), jnp.float32), 0.5, 1.5).astype(jnp.bfloat16),
        "norm_query": jnp.clip(1.0 + 0.15 * jax.random.normal(splits[12], (HEAD_SIZE,), jnp.float32), 0.25, 1.75).astype(jnp.bfloat16),
        "norm_key": jnp.clip(1.0 + 0.15 * jax.random.normal(splits[13], (HEAD_SIZE,), jnp.float32), 0.25, 1.75).astype(jnp.bfloat16),
        "cont_lengths": jax.vmap(lambda own: uneven(own, NCONT, PROMPT_TOKENS, CONT_MAX, 1))(jax.random.split(splits[14], PROMPT_GROUPS * (GROUP_DEVICES - 1) * MICRO_BATCHES)).reshape((PROMPT_GROUPS, GROUP_DEVICES - 1, MICRO_BATCHES, NCONT)).astype(jnp.int32),
    }


eps = 1e-06
rope_base = 1000000.0
masked = -1e+30
highest_precision = lax.Precision.HIGHEST

@jax.custom_vjp
def low(v):
    return lax.optimization_barrier(v.astype(jnp.bfloat16)).astype(jnp.float32)

@jax.custom_vjp
def low_back(v):
    return v

def low_keep(v):
    return (low(v), None)

def low_pass(kept, grad):
    return (grad,)

def back_keep(v):
    return (v, None)

def back_low(kept, grad):
    return (low(grad),)
low.defvjp(low_keep, low_pass)
low_back.defvjp(back_keep, back_low)

def apply_norm(values, gain):
    return values * lax.rsqrt(lax.optimization_barrier(jnp.mean(values * values, axis=-1, keepdims=True)) + eps) * gain

def apply_rotary(values, cosine_rows, sine_table):
    half_dim = values.shape[-1] // 2
    leading = values[..., :half_dim]
    trailing = values[..., half_dim:]
    return jnp.concatenate([leading * cosine_rows - trailing * sine_table, trailing * cosine_rows + leading * sine_table], axis=-1)

def matmul(left_side, right_side):
    return jnp.dot(left_side, right_side, precision=highest_precision)

def layout(cont_lengths):
    seg_ends = jnp.cumsum(cont_lengths, axis=-1, dtype=jnp.int32)
    starts = seg_ends - cont_lengths
    row_ids = jnp.arange(PROMPT_TOKENS, dtype=jnp.int32)
    seg_index = lax.optimization_barrier(jnp.sum((row_ids[:, None] >= seg_ends[..., None, :]).astype(jnp.int32), axis=-1, dtype=jnp.int32))
    seg_onehot = seg_index[..., None] == jnp.arange(NCONT, dtype=jnp.int32)
    seg_start = lax.optimization_barrier(jnp.sum(jnp.where(seg_onehot, starts[..., None, :], 0), axis=-1, dtype=jnp.int32))
    cont_pos = PROMPT_TOKENS + row_ids - seg_start
    device_base = NCONT * jnp.arange(GROUP_DEVICES - 1, dtype=jnp.int32)
    cont_seg = 1 + seg_index + device_base[None, :, None, None]
    prompt_pos = jnp.broadcast_to(row_ids, (PROMPT_GROUPS, 1, MICRO_BATCHES, PROMPT_TOKENS)).astype(jnp.int32)
    prompt_seg = jnp.zeros((PROMPT_GROUPS, 1, MICRO_BATCHES, PROMPT_TOKENS), jnp.int32)
    rank_pos = jnp.concatenate([prompt_pos, cont_pos.astype(jnp.int32)], axis=1)
    rank_seg = jnp.concatenate([prompt_seg, cont_seg.astype(jnp.int32)], axis=1)
    holders = jnp.where(jnp.arange(MICRO_BATCHES, dtype=jnp.int32) % 2 == 1, GROUP_DEVICES - 1, 0).astype(jnp.int32)
    ranks = jnp.bitwise_xor(jnp.arange(GROUP_DEVICES, dtype=jnp.int32)[:, None], holders[None, :]).astype(jnp.int32)
    picker = jnp.broadcast_to(ranks[None, :, :, None], (PROMPT_GROUPS, GROUP_DEVICES, MICRO_BATCHES, PROMPT_TOKENS)).astype(jnp.int32)
    position = jnp.take_along_axis(rank_pos, picker, axis=1)
    segment = jnp.take_along_axis(rank_seg, picker, axis=1)
    return (position, segment)

def attend_block(operands):
    block_queries, block_keys, block_values, seg_block, pos_block = operands
    unscaled_scores = jnp.einsum('mhzk,ihk->hzmi', block_queries, block_keys, precision=highest_precision) * HEAD_SIZE ** (-0.5)
    scores = low_back(unscaled_scores)
    allowed = (seg_block[None, :] == 0) & (seg_block[:, None] != 0) | (seg_block[:, None] == seg_block[None, :]) & (pos_block[None, :] <= pos_block[:, None])
    scores = jnp.where(allowed[None, None], scores, masked)
    probabilities = jax.nn.softmax(scores, axis=-1)
    return low_back(jnp.einsum('ycxu,uyi->xyci', low(probabilities), block_values, precision=highest_precision))

def reference(tokens, cotangent, query_weight, key_matrix, value_matrix, head_gate_weight, out_weight, gate_weight, up_weight, down_weight, norm_attn, norm_mlp, norm_query, norm_key, cont_lengths):
    position, segment = layout(cont_lengths)
    token_pos = position.reshape(TOKEN_COUNT)
    block_length = GROUP_DEVICES * PROMPT_TOKENS
    seg_blocks = segment.transpose(0, 2, 1, 3).reshape(PROMPT_GROUPS * MICRO_BATCHES, block_length)
    pos_blocks = position.transpose(0, 2, 1, 3).reshape(PROMPT_GROUPS * MICRO_BATCHES, block_length)
    inverse = jnp.power(rope_base, -jnp.arange(HEAD_SIZE // 2, dtype=jnp.float32) * (2.0 / HEAD_SIZE))
    angles = token_pos.astype(jnp.float32)[:, None] * inverse[None, :]
    cosine_rows = jnp.cos(angles)[:, None, :]
    sine_table = jnp.sin(angles)[:, None, :]
    repeat_heads = QUERY_HEADS // KEY_HEADS

    def layer(inputs, query_full, key_full, value_full, head_gate_full, out_full, gate_full, up_full, down_full, gain_attn, gain_mlp, gain_query, key_gain):
        normed_one = low(apply_norm(inputs, gain_attn))
        query_proj = low_back(matmul(normed_one, query_full))
        projected_keys = low_back(matmul(normed_one, key_full))
        projected_values = low_back(matmul(normed_one, value_full))
        gate_logit = low_back(matmul(normed_one, head_gate_full))
        rotated_queries = low(apply_rotary(apply_norm(query_proj.reshape(TOKEN_COUNT, QUERY_HEADS, HEAD_SIZE), gain_query), cosine_rows, sine_table))
        rotated_keys = low(apply_rotary(apply_norm(projected_keys.reshape(TOKEN_COUNT, KEY_HEADS, HEAD_SIZE), key_gain), cosine_rows, sine_table))
        values_lower = low(projected_values).reshape(TOKEN_COUNT, KEY_HEADS, HEAD_SIZE)
        queries_per_block = rotated_queries.reshape(PROMPT_GROUPS, GROUP_DEVICES, MICRO_BATCHES, PROMPT_TOKENS, KEY_HEADS, repeat_heads, HEAD_SIZE).transpose(0, 2, 1, 3, 4, 5, 6).reshape(PROMPT_GROUPS * MICRO_BATCHES, block_length, KEY_HEADS, repeat_heads, HEAD_SIZE)
        keys_per_block = rotated_keys.reshape(PROMPT_GROUPS, GROUP_DEVICES, MICRO_BATCHES, PROMPT_TOKENS, KEY_HEADS, HEAD_SIZE).transpose(0, 2, 1, 3, 4, 5).reshape(PROMPT_GROUPS * MICRO_BATCHES, block_length, KEY_HEADS, HEAD_SIZE)
        values_per_block = values_lower.reshape(PROMPT_GROUPS, GROUP_DEVICES, MICRO_BATCHES, PROMPT_TOKENS, KEY_HEADS, HEAD_SIZE).transpose(0, 2, 1, 3, 4, 5).reshape(PROMPT_GROUPS * MICRO_BATCHES, block_length, KEY_HEADS, HEAD_SIZE)
        attended = lax.map(jax.checkpoint(attend_block), (queries_per_block, keys_per_block, values_per_block, seg_blocks, pos_blocks))
        attended = attended.reshape(PROMPT_GROUPS, MICRO_BATCHES, GROUP_DEVICES, PROMPT_TOKENS, QUERY_HEADS, HEAD_SIZE).transpose(0, 2, 1, 3, 4, 5).reshape(TOKEN_COUNT, QUERY_HEADS, HEAD_SIZE)
        head_gate = jax.nn.sigmoid(gate_logit)
        gated = low((attended * head_gate[:, :, None]).reshape(TOKEN_COUNT, QUERY_HEADS * HEAD_SIZE))
        middle = inputs + low_back(matmul(gated, out_full))
        normed_two = low(apply_norm(middle, gain_mlp))
        gate_pre = low_back(matmul(normed_two, gate_full))
        up_pre = low_back(matmul(normed_two, up_full))
        hidden = low(jax.nn.silu(gate_pre) * up_pre)
        return middle + low_back(matmul(hidden, down_full))
    result, pullback = jax.vjp(layer, tokens.astype(jnp.float32), query_weight.astype(jnp.float32), key_matrix.astype(jnp.float32), value_matrix.astype(jnp.float32), head_gate_weight.astype(jnp.float32), out_weight.astype(jnp.float32), gate_weight.astype(jnp.float32), up_weight.astype(jnp.float32), down_weight.astype(jnp.float32), norm_attn.astype(jnp.float32), norm_mlp.astype(jnp.float32), norm_query.astype(jnp.float32), norm_key.astype(jnp.float32))
    grads = pullback(cotangent.astype(jnp.float32))
    return (result.astype(jnp.bfloat16), grads[0], grads[1], grads[2], grads[3], grads[4], grads[5], grads[6], grads[7], grads[8], grads[9], grads[10], grads[11], grads[12])
```

```python
import jax
import jax.numpy as jnp
from jax import lax
from jax.sharding import PartitionSpec as P

MICRO_BATCHES = 2
GROUP_DEVICES = 4

eps = 1e-06
rope_base = 1000000.0
masked = -1e30
f32 = jnp.float32
bf16 = jnp.bfloat16


def product(left_side, right_side):
    return jnp.dot(left_side, right_side, preferred_element_type=f32)


def by_transpose(left_side, right_side):
    return lax.dot_general(
        left_side, right_side, (((1,), (1,)), ((), ())), preferred_element_type=f32
    )


def transpose_by(left_side, right_side):
    return lax.dot_general(
        left_side, right_side, (((0,), (0,)), ((), ())), preferred_element_type=f32
    )


def recip_rms(values):
    return lax.rsqrt(jnp.mean(values * values, axis=-1, keepdims=True) + eps)


def rms_back(values, reciprocal, gain, gradient):
    scaled = gain * gradient
    cubed = reciprocal * reciprocal * reciprocal
    back = reciprocal * scaled - values * cubed * jnp.mean(scaled * values, axis=-1, keepdims=True)
    return (back, gradient * values * reciprocal)


def apply_rotary(values, cosine_rows, sine_table):
    half_dim = values.shape[-1] // 2
    leading = values[..., :half_dim]
    trailing = values[..., half_dim:]
    return jnp.concatenate(
        [
            leading * cosine_rows - trailing * sine_table,
            trailing * cosine_rows + leading * sine_table,
        ],
        axis=-1,
    )


def layout(lengths, relative, row_count):
    seg_ends = jnp.cumsum(lengths, dtype=jnp.int32)
    starts = seg_ends - lengths
    row_ids = jnp.arange(row_count, dtype=jnp.int32)
    seg_index = jnp.sum(
        (row_ids[:, None] >= seg_ends[None, :]).astype(jnp.int32), axis=1, dtype=jnp.int32
    )
    seg_onehot = seg_index[:, None] == jnp.arange(lengths.shape[0], dtype=jnp.int32)[None, :]
    seg_start = jnp.sum(jnp.where(seg_onehot, starts[None, :], 0), axis=1, dtype=jnp.int32)
    prompt = relative == 0
    segment = jnp.where(prompt, 0, 1 + seg_index)
    position = jnp.where(prompt, row_ids, row_count + row_ids - seg_start)
    return (segment, position)


def ring_order(count):
    return list(range(0, count, 2)) + list(range(count - 1, 0, -2))


def ring_step(block, count, forward):
    order = ring_order(count)
    turn = 1 if forward else -1
    route = [(order[i], order[(i + turn) % count]) for i in range(count)]
    return lax.ppermute(block, "dp", route)


def after(block, *earlier):
    return lax.optimization_barrier((block,) + earlier)[0]


def ring_gather(block, count, far_forward, gate=None):
    half = count // 2
    ahead, behind = [block], [block]
    if gate is not None:
        ahead[0] = behind[0] = after(block, gate)
    for step in range(1, half + 1):
        if step < half or far_forward:
            ahead.append(ring_step(ahead[-1], count, True))
        if step < half or not far_forward:
            behind.append(ring_step(behind[-1], count, False))
    slots = [ahead[step] for step in range(half - 1, -1, -1)]
    slots += [behind[step] for step in range(1, half)]
    slots.append(ahead[half] if far_forward else behind[half])
    return slots, (ahead, behind)


def ring_scatter(chunk, count, far_forward):
    half = count // 2
    own = half - 1
    ahead = behind = None
    for step in range(half, 0, -1):
        if step < half or far_forward:
            slot = own + step
            part = chunk(slot)
            if ahead is not None:
                part = part + ahead.astype(f32)
            ahead = ring_step(part.astype(bf16), count, True)
        if step < half or not far_forward:
            slot = own - step if step < half else count - 1
            part = chunk(slot)
            if behind is not None:
                part = part + behind.astype(f32)
            behind = ring_step(part.astype(bf16), count, False)
    return chunk(own) + ahead.astype(f32) + behind.astype(f32)


def swap_core(block):
    return lax.ppermute(block, "mp", [(i, i ^ 1) for i in range(lax.axis_size("mp"))])


def swap_x(block):
    return lax.ppermute(block, "mp", [(i, i ^ 2) for i in range(lax.axis_size("mp"))])


def sum_devices(values, levels_mp):
    for level in levels_mp:
        values = values + lax.ppermute(
            values, "mp", [(i, i ^ level) for i in range(lax.axis_size("mp"))]
        )
    count = lax.axis_size("dp")
    level = 1
    while level < count:
        values = values + lax.ppermute(values, "dp", [(i, i ^ level) for i in range(count)])
        level *= 2
    return values


def across(other_part, own_part):
    chip = (own_part + swap_core(other_part.astype(bf16)).astype(f32)).astype(bf16)
    return chip.astype(f32) + swap_x(chip).astype(f32)


def group_route(apart, sources):
    count = lax.axis_size("dp")
    route = []
    for base in range(0, count, GROUP_DEVICES):
        route += [(base + s, base + (s ^ apart)) for s in sources]
    return route


def scores_of(grouped_queries, gathered_keys, allowed, score_scale):
    unscaled_scores = (
        jnp.einsum("mhzk,ihk->hzmi", grouped_queries, gathered_keys, preferred_element_type=f32)
        * score_scale
    )
    return jnp.where(allowed[None, None], unscaled_scores, masked)


def on_device(
    tokens,
    cotangent,
    query_weight,
    key_matrix,
    value_matrix,
    head_gate_weight,
    out_weight,
    gate_weight,
    up_weight,
    down_weight,
    norm_attn,
    norm_mlp,
    norm_query,
    norm_key,
    cont_lengths,
):
    count = lax.axis_size("dp")
    dp_index = lax.axis_index("dp")
    core = lax.axis_index("mp") % 2
    place = jnp.where(dp_index % 2 == 0, dp_index // 2, count - 1 - dp_index // 2)
    offset = dp_index % GROUP_DEVICES
    group_index = dp_index // GROUP_DEVICES
    total_rows, width = tokens.shape
    block_rows = total_rows // MICRO_BATCHES
    own_rows = block_rows // 2
    depth = width // count
    head_dim = norm_query.shape[0]
    head_count = head_gate_weight.shape[1]
    query_cols = query_weight.shape[1]
    key_cols = key_matrix.shape[1]
    kv_heads = key_cols // head_dim
    repeat_heads = head_count // kv_heads
    hidden_units = gate_weight.shape[1]
    score_scale = head_dim ** (-0.5)
    gain_query = norm_query.astype(f32)
    key_gain = norm_key.astype(f32)
    first_place = (place + count - (count // 2 - 1)) % count
    order = ring_order(count)

    extra = 128
    packed = jnp.concatenate(
        [
            query_weight,
            key_matrix,
            value_matrix,
            head_gate_weight,
            norm_attn[:, None],
            norm_mlp[:, None],
            jnp.zeros((depth, extra - head_count - 2), bf16),
        ],
        axis=1,
    )
    in_slots, in_steps = ring_gather(packed, count, False)
    out_slots, out_steps = ring_gather(out_weight, count, False, in_steps[0][1])
    gate_slots, gate_steps = ring_gather(gate_weight, count, True, in_steps[0][2])
    up_slots, up_steps = ring_gather(up_weight, count, False, in_steps[0][3])
    down_slots, _ = ring_gather(down_weight, count, True, gate_steps[0][2])
    in_full = jnp.concatenate(in_slots, axis=0)
    out_full = jnp.concatenate(out_slots, axis=1)
    gate_up_full = jnp.concatenate(
        [jnp.concatenate([g, u], axis=1) for g, u in zip(gate_slots, up_slots)], axis=0
    )
    down_full = jnp.concatenate(down_slots, axis=1)
    first_gain = query_cols + 2 * key_cols + head_count
    gain_attn = in_full[:, first_gain].astype(f32)[None, :]
    gain_mlp = in_full[:, first_gain + 1].astype(f32)[None, :]

    def columns_in(block):
        ring = [block[:, i * depth : (i + 1) * depth] for i in order]
        return lax.dynamic_slice_in_dim(
            jnp.concatenate(ring + ring, axis=1), first_place * depth, width, axis=1
        )

    def columns_out(block):
        twice = jnp.concatenate([block, block], axis=1)
        back = lax.dynamic_slice_in_dim(
            twice, ((count - first_place) % count) * depth, width, axis=1
        )
        where_of = {device: i for i, device in enumerate(order)}
        return jnp.concatenate(
            [back[:, where_of[i] * depth : (where_of[i] + 1) * depth] for i in range(count)],
            axis=1,
        )

    def rows_in(block):
        halves = block.reshape((MICRO_BATCHES, 2, own_rows) + block.shape[1:])
        swapped = jnp.concatenate([halves[:, 1:], halves[:, :1]], axis=1)
        return jnp.where(core == 0, halves, swapped).reshape(block.shape)

    def rows_out(own, other):
        low = jnp.where(core == 0, own, other)
        high = jnp.where(core == 0, other, own)
        return jnp.stack([low, high], axis=1).reshape(total_rows, width)

    inputs_low = columns_in(rows_in(tokens))
    upstream_low = columns_in(rows_in(cotangent))
    inputs = inputs_low.astype(f32)

    inverse = jnp.power(rope_base, -jnp.arange(head_dim // 2, dtype=f32) * (2.0 / head_dim))
    relatives, segments, positions = [], [], []
    for micro in range(MICRO_BATCHES):
        holder = GROUP_DEVICES - 1 if micro % 2 == 1 else 0
        relative = jnp.bitwise_xor(offset, holder)
        lengths = cont_lengths[group_index, jnp.maximum(relative - 1, 0), micro]
        segment, position = layout(lengths, relative, block_rows)
        relatives.append(relative)
        segments.append(segment)
        positions.append(position)
    segment = rows_in(jnp.concatenate(segments))
    position = rows_in(jnp.concatenate(positions))
    angles = position.astype(f32)[:, None] * inverse[None, :]
    cosine_rows = jnp.cos(angles)[:, None, :]
    sine_table = jnp.sin(angles)[:, None, :]

    recip_one = recip_rms(inputs)
    normed_one = (inputs * recip_one * gain_attn).astype(bf16)
    projected = product(normed_one, in_full)
    query_heads = projected[:, :query_cols].reshape(total_rows, head_count, head_dim)
    key_heads = projected[:, query_cols : query_cols + key_cols].reshape(
        total_rows, kv_heads, head_dim
    )
    values_lower = projected[:, query_cols + key_cols : query_cols + 2 * key_cols].astype(bf16)
    gate_logit = projected[:, query_cols + 2 * key_cols : query_cols + 2 * key_cols + head_count]
    recip_query = recip_rms(query_heads)
    recip_key = recip_rms(key_heads)
    rotated_queries = apply_rotary(
        query_heads * recip_query * gain_query, cosine_rows, sine_table
    ).astype(bf16)
    rotated_keys = (
        apply_rotary(key_heads * recip_key * key_gain, cosine_rows, sine_table)
        .astype(bf16)
        .reshape(total_rows, key_cols)
    )
    own_kv = jnp.concatenate([rotated_keys, values_lower], axis=1)

    first_kv, second_kv = own_kv[:block_rows], own_kv[block_rows:]
    sent = jnp.where(offset == 0, first_kv, second_kv)
    by_one = lax.ppermute(sent, "dp", group_route(1, (0, 3)))
    by_two = lax.ppermute(sent, "dp", group_route(2, (0, 3)))
    by_both = lax.ppermute(by_one, "dp", group_route(2, (1, 2)))
    far_kv = [
        jnp.where(offset == 1, by_one, jnp.where(offset == 2, by_two, by_both)),
        jnp.where(offset == 2, by_one, jnp.where(offset == 1, by_two, by_both)),
    ]

    head_gate = jax.nn.sigmoid(gate_logit)
    attention = []
    for micro in range(MICRO_BATCHES):
        rows = slice(micro * block_rows, (micro + 1) * block_rows)
        seg, pos = segment[rows], position[rows]
        own_mask = (seg[:, None] == seg[None, :]) & (pos[None, :] <= pos[:, None])
        far_mask = jnp.broadcast_to(
            jnp.logical_not(relatives[micro] == 0), (block_rows, block_rows)
        )
        allowed = jnp.concatenate([far_mask, own_mask], axis=1)
        all_kv = jnp.concatenate([far_kv[micro], own_kv[rows]], axis=0)
        gathered_keys = all_kv[:, :key_cols].reshape(2 * block_rows, kv_heads, head_dim)
        gathered_values = all_kv[:, key_cols:].reshape(2 * block_rows, kv_heads, head_dim)
        grouped_queries = rotated_queries[rows].reshape(
            block_rows, kv_heads, repeat_heads, head_dim
        )
        scores = scores_of(grouped_queries, gathered_keys, allowed, score_scale)
        row_peak = jnp.max(scores, axis=-1, keepdims=True)
        exponent = jnp.exp(scores - row_peak)
        row_total = jnp.sum(exponent, axis=-1, keepdims=True)
        probabilities_lower = (exponent / row_total).astype(bf16)
        log_total = row_peak + jnp.log(row_total)
        attended = jnp.einsum(
            "ycxu,uyi->xyci", probabilities_lower, gathered_values, preferred_element_type=f32
        ).reshape(block_rows, head_count, head_dim)
        gated_low = (
            (attended * head_gate[rows][:, :, None])
            .reshape(block_rows, head_count * head_dim)
            .astype(bf16)
        )
        attention.append(
            (allowed, gathered_keys, gathered_values, grouped_queries, log_total, attended, gated_low)
        )

    middles, recips_two, norms_two = [], [], []
    for micro in range(MICRO_BATCHES):
        base = micro * block_rows
        gated_low = attention[micro][6]
        summed = across(
            product(gated_low[own_rows:], out_full), product(gated_low[:own_rows], out_full)
        )
        middle = inputs[base : base + own_rows] + summed
        recip_two = recip_rms(middle)
        own_norm = (middle * recip_two * gain_mlp).astype(bf16)
        middles.append(middle)
        recips_two.append(recip_two)
        norms_two += [own_norm, swap_core(own_norm)]
    normed_two = jnp.concatenate(norms_two, axis=0)
    pre = product(normed_two, gate_up_full)
    gate_pre, up_pre = pre[:, :hidden_units], pre[:, hidden_units:]
    sigmoid_gate = jax.nn.sigmoid(gate_pre)
    swish_gate = gate_pre * sigmoid_gate
    hidden_low = (swish_gate * up_pre).astype(bf16)
    down_grad = ring_scatter(
        lambda slot: transpose_by(hidden_low, upstream_low[:, slot * depth : (slot + 1) * depth]),
        count,
        True,
    )
    hidden_grad = by_transpose(upstream_low, down_full)
    gate_grad = (
        hidden_grad * up_pre * sigmoid_gate * (1.0 + gate_pre * (1.0 - sigmoid_gate))
    ).astype(bf16)
    up_grad = (hidden_grad * swish_gate).astype(bf16)
    gate_up_grad = jnp.concatenate([gate_grad, up_grad], axis=1)
    gate_weight_grad = ring_scatter(
        lambda slot: transpose_by(normed_two[:, slot * depth : (slot + 1) * depth], gate_grad),
        count,
        True,
    )
    up_weight_grad = ring_scatter(
        lambda slot: transpose_by(normed_two[:, slot * depth : (slot + 1) * depth], up_grad),
        count,
        False,
    )
    layer_rows, middle_grads, middle_lows = [], [], []
    mlp_gain_grad = 0.0
    for micro in range(MICRO_BATCHES):
        base = micro * block_rows
        own, other = slice(base, base + own_rows), slice(base + own_rows, base + block_rows)
        summed = across(
            by_transpose(gate_up_grad[other], gate_up_full),
            by_transpose(gate_up_grad[own], gate_up_full),
        )
        middle_back, gain_terms = rms_back(middles[micro], recips_two[micro], gain_mlp, summed)
        mlp_gain_grad = mlp_gain_grad + jnp.sum(gain_terms, axis=0)
        middle_grad = upstream_low[own].astype(f32) + middle_back
        middle_grads.append(middle_grad)
        own_low = middle_grad.astype(bf16)
        middle_lows += [own_low, swap_core(own_low)]
    middle_low = jnp.concatenate(middle_lows, axis=0)
    for micro in range(MICRO_BATCHES):
        base = micro * block_rows
        own, other = slice(base, base + own_rows), slice(base + own_rows, base + block_rows)
        mlp_out = across(product(hidden_low[other], down_full), product(hidden_low[own], down_full))
        layer_rows.append(columns_out((middles[micro] + mlp_out).astype(bf16)))
    layer_own = jnp.stack(layer_rows)
    layer_out = rows_out(layer_own, swap_core(layer_own))

    gated_all = jnp.concatenate([a[6] for a in attention], axis=0)
    out_weight_grad = ring_scatter(
        lambda slot: transpose_by(gated_all, middle_low[:, slot * depth : (slot + 1) * depth]),
        count,
        False,
    )
    logit_grads, query_rot_grads, key_grads, value_grads = [], [], [], []
    for micro in range(MICRO_BATCHES):
        rows = slice(micro * block_rows, (micro + 1) * block_rows)
        (allowed, gathered_keys, gathered_values, grouped_queries, log_total, attended, _) = (
            attention[micro]
        )
        gate = head_gate[rows]
        gated_grad = by_transpose(middle_low[rows], out_full).reshape(
            block_rows, head_count, head_dim
        )
        attended_low = (gated_grad * gate[:, :, None]).astype(bf16)
        logit_grads.append(
            (jnp.sum(gated_grad * attended, axis=-1) * gate * (1.0 - gate)).astype(bf16)
        )
        again = scores_of(grouped_queries, gathered_keys, allowed, score_scale)
        probs_again = jnp.exp(again - log_total)
        group_gradient = attended_low.reshape(block_rows, kv_heads, repeat_heads, head_dim)
        prob_grad = jnp.einsum(
            "mhzk,ihk->hzmi", group_gradient, gathered_values, preferred_element_type=f32
        )
        scores_gradient = (
            probs_again * (prob_grad - jnp.sum(probs_again * prob_grad, axis=-1, keepdims=True))
        ).astype(bf16)
        query_rot_grads.append(
            jnp.einsum(
                "ycxu,uyi->xyci", scores_gradient, gathered_keys, preferred_element_type=f32
            ).reshape(block_rows, head_count, head_dim)
            * score_scale
        )
        key_grads.append(
            jnp.einsum(
                "jcuk,ujca->kja", scores_gradient, grouped_queries, preferred_element_type=f32
            ).reshape(2 * block_rows, key_cols)
            * score_scale
        )
        value_grads.append(
            jnp.einsum(
                "jcuk,ujca->kja",
                probs_again.astype(bf16),
                group_gradient,
                preferred_element_type=f32,
            ).reshape(2 * block_rows, key_cols)
        )
    far_grads = [
        jnp.concatenate([k[:block_rows], v[:block_rows]], axis=1)
        for k, v in zip(key_grads, value_grads)
    ]
    by_both = lax.ppermute(
        jnp.where(offset == 3, far_grads[0], far_grads[1]).astype(bf16),
        "dp",
        group_route(2, (0, 3)),
    ).astype(f32)
    by_two = lax.ppermute(
        jnp.where(offset == 2, far_grads[0], far_grads[1]).astype(bf16),
        "dp",
        group_route(2, (1, 2)),
    ).astype(f32)
    by_one = lax.ppermute(
        (jnp.where(offset == 1, far_grads[0], far_grads[1]) + by_both).astype(bf16),
        "dp",
        group_route(1, (1, 2)),
    ).astype(f32)
    arrived = by_one + by_two
    key_rot_grads, value_lows = [], []
    for micro in range(MICRO_BATCHES):
        prompt = relatives[micro] == 0
        back = jnp.where(prompt, arrived, 0.0)
        key_rot_grads.append(key_grads[micro][block_rows:] + back[:, :key_cols])
        value_lows.append((value_grads[micro][block_rows:] + back[:, key_cols:]).astype(bf16))
    query_grad, query_gain_terms = rms_back(
        query_heads,
        recip_query,
        gain_query,
        apply_rotary(jnp.concatenate(query_rot_grads, axis=0), cosine_rows, -sine_table),
    )
    key_grad, key_gain_terms = rms_back(
        key_heads,
        recip_key,
        key_gain,
        apply_rotary(
            jnp.concatenate(key_rot_grads, axis=0).reshape(total_rows, kv_heads, head_dim),
            cosine_rows,
            -sine_table,
        ),
    )
    head_gains = jnp.stack(
        [jnp.sum(query_gain_terms, axis=(0, 1)), jnp.sum(key_gain_terms, axis=(0, 1))]
    )
    head_gains = sum_devices(head_gains, (1, 2))
    in_grad = jnp.concatenate(
        [
            query_grad.reshape(total_rows, query_cols).astype(bf16),
            key_grad.reshape(total_rows, key_cols).astype(bf16),
            jnp.concatenate(value_lows, axis=0),
            jnp.concatenate(logit_grads, axis=0),
            jnp.zeros((total_rows, extra - head_count), bf16),
        ],
        axis=1,
    )
    in_weight_grad = ring_scatter(
        lambda slot: transpose_by(normed_one[:, slot * depth : (slot + 1) * depth], in_grad),
        count,
        False,
    )
    attn_gain_grad = 0.0
    input_rows = []
    for micro in range(MICRO_BATCHES):
        base = micro * block_rows
        own, other = slice(base, base + own_rows), slice(base + own_rows, base + block_rows)
        summed = across(
            by_transpose(in_grad[other], in_full), by_transpose(in_grad[own], in_full)
        )
        input_back, gain_terms = rms_back(inputs[own], recip_one[own], gain_attn, summed)
        attn_gain_grad = attn_gain_grad + jnp.sum(gain_terms, axis=0)
        input_rows.append(columns_out(middle_grads[micro] + input_back))
    input_own = jnp.stack(input_rows)
    tokens_grad = rows_out(input_own, swap_core(input_own))
    gains = columns_out(jnp.stack([attn_gain_grad, mlp_gain_grad]))
    gains = sum_devices(gains, (1,))
    gains = lax.dynamic_slice_in_dim(gains, dp_index * depth, depth, axis=1)
    return (
        layer_out,
        tokens_grad,
        in_weight_grad[:, :query_cols],
        in_weight_grad[:, query_cols : query_cols + key_cols],
        in_weight_grad[:, query_cols + key_cols : query_cols + 2 * key_cols],
        in_weight_grad[:, query_cols + 2 * key_cols : query_cols + 2 * key_cols + head_count],
        out_weight_grad,
        gate_weight_grad,
        up_weight_grad,
        down_grad,
        gains[0],
        gains[1],
        head_gains[0],
        head_gains[1],
    )


def solution(mesh):
    rows, weight, turned = P("dp", None), P("dp", "mp"), P("mp", "dp")
    weights = (weight, weight, weight, weight, turned, weight, weight, turned)
    placed = (rows, rows) + weights + (P("dp"), P("dp"), P(), P())
    return jax.shard_map(
        on_device, mesh=mesh, in_specs=placed + (P(),), out_specs=placed, check_vma=False
    )
```

```python
import functools

import jax
import jax.numpy as jnp
from jax import lax
from jax.experimental import pallas as pl
from jax.experimental.pallas import tpu as pltpu
from jax.sharding import PartitionSpec as P

MICRO_BATCHES = 2
GROUP_DEVICES = 4

eps = 1e-06
rope_base = 1000000.0
masked = -1e30
f32 = jnp.float32
bf16 = jnp.bfloat16


def product(left_side, right_side):
    return jnp.dot(left_side, right_side, preferred_element_type=f32)


def by_transpose(left_side, right_side):
    return lax.dot_general(
        left_side, right_side, (((1,), (1,)), ((), ())), preferred_element_type=f32
    )


def transpose_by(left_side, right_side):
    return lax.dot_general(
        left_side, right_side, (((0,), (0,)), ((), ())), preferred_element_type=f32
    )


def recip_rms(values):
    return lax.rsqrt(jnp.mean(values * values, axis=-1, keepdims=True) + eps)


def rms_back(values, reciprocal, gain, gradient):
    scaled = gain * gradient
    cubed = reciprocal * reciprocal * reciprocal
    back = reciprocal * scaled - values * cubed * jnp.mean(scaled * values, axis=-1, keepdims=True)
    return (back, gradient * values * reciprocal)


def layout(lengths, relative, row_count):
    seg_ends = jnp.cumsum(lengths, dtype=jnp.int32)
    starts = seg_ends - lengths
    row_ids = jnp.arange(row_count, dtype=jnp.int32)
    seg_index = jnp.sum(
        (row_ids[:, None] >= seg_ends[None, :]).astype(jnp.int32), axis=1, dtype=jnp.int32
    )
    seg_onehot = seg_index[:, None] == jnp.arange(lengths.shape[0], dtype=jnp.int32)[None, :]
    seg_start = jnp.sum(jnp.where(seg_onehot, starts[None, :], 0), axis=1, dtype=jnp.int32)
    prompt = relative == 0
    segment = jnp.where(prompt, 0, 1 + seg_index)
    position = jnp.where(prompt, row_ids, row_count + row_ids - seg_start)
    return (segment, position)


def ring_order(count):
    return list(range(0, count, 2)) + list(range(count - 1, 0, -2))


def ring_step(block, count, forward):
    places = ring_order(count)
    turn = 1 if forward else -1
    route = [(places[i], places[(i + turn) % count]) for i in range(count)]
    return lax.ppermute(block, "dp", route)


class Gather:
    def __init__(self, block, count):
        self.count = count
        self.left = count // 2
        self.cut = (block.shape[1] // 256) * 128
        self.held = [[block], [block]]
        self.flying = []

    def issue(self):
        if self.left:
            self.left -= 1
            ahead, behind = self.held[0][-1], self.held[1][-1]
            if not self.left:
                ahead, behind = ahead[:, : self.cut], behind[:, self.cut :]
            self.flying = [
                (0, ring_step(ahead, self.count, True)),
                (1, ring_step(behind, self.count, False)),
            ]

    def land(self, arrays):
        for (way, _), array in zip(self.flying, arrays):
            self.held[way].append(array)
        self.flying = []

    def gathered(self, first, end):
        ahead, behind = self.held
        half = self.count // 2
        near = [ahead[step] for step in range(half - 1, -1, -1)]
        near += [behind[step] for step in range(1, half)]
        near.append(jnp.concatenate([ahead[half], behind[half]], axis=1))
        return jnp.concatenate([block[:, first:end] for block in near], axis=0)


class Scatter:
    def __init__(self, chunk, count, split=True):
        half = count // 2
        self.count, self.chunk, self.split = count, chunk, split
        self.own = half - 1
        self.left = half
        self.got = [None, None]
        self.flying = []

    def issue(self, *values):
        parts = []
        if self.left == self.count // 2:
            far = self.chunk(self.own + self.left).astype(bf16)
            cut = far.shape[1] // 256 * 128 or far.shape[1] // 2
            if self.split:
                parts = [(0, far[:, :cut]), (1, far[:, cut:])]
            else:
                ahead = self.chunk(self.own + self.left - 1).astype(bf16)
                parts = [(0, ahead), (1, far)]
        elif self.left > 0:
            late = 0 if self.split else 1
            for way, slot in ((0, self.own + self.left - late), (1, self.own - self.left)):
                if slot == self.own:
                    self.kept = self.got[way]
                    continue
                part, got = self.chunk(slot), self.got[way].astype(f32)
                lack = part.shape[1] - got.shape[1]
                if lack:
                    got = jnp.pad(got, ((0, 0), ((0, lack), (lack, 0))[way]))
                parts.append((way, (part + got).astype(bf16)))
        self.left -= 1
        if parts and values:
            tied = lax.optimization_barrier(tuple(part for _, part in parts) + values)
            parts = [(way, part) for (way, _), part in zip(parts, tied)]
            values = tied[len(parts) :]
        self.flying = [(way, ring_step(part, self.count, way == 0)) for way, part in parts]
        return values

    def land(self, arrays):
        for (way, _), array in zip(self.flying, arrays):
            self.got[way] = array
        self.flying = []

    def total(self):
        if not self.split:
            self.got[0] = self.kept
        return self.chunk(self.own) + self.got[0].astype(f32) + self.got[1].astype(f32)


def single(values):
    return values[0] if len(values) == 1 else values


def pump(ring, *values):
    arrays = [array for _, array in ring.flying]
    if arrays and values:
        tied = lax.optimization_barrier(tuple(arrays) + values)
        arrays, values = list(tied[: len(arrays)]), tied[len(arrays) :]
    ring.land(arrays)
    if isinstance(ring, Scatter):
        values = ring.issue(*values)
    else:
        ring.issue()
    return single(values)


def settle(ring, *values):
    arrays = [array for _, array in ring.flying]
    tied = lax.optimization_barrier(tuple(arrays) + values)
    ring.land(list(tied[: len(arrays)]))
    return single(tied[len(arrays) :])


def drain(ring, *values):
    while ring.flying or ring.left > 0:
        values = pump(ring, *values)
        values = values if isinstance(values, tuple) else (values,)
    return single(values)


def order(*values):
    return lax.optimization_barrier(values)


def swap_core(block):
    return lax.ppermute(block, "mp", [(i, i ^ 1) for i in range(lax.axis_size("mp"))])


def swap_x(block):
    return lax.ppermute(block, "mp", [(i, i ^ 2) for i in range(lax.axis_size("mp"))])


def swap_dp(block, level):
    count = lax.axis_size("dp")
    return lax.ppermute(block, "dp", [(i, i ^ level) for i in range(count)])


def chip_sum(other_part, own_part):
    return (own_part + swap_core(other_part.astype(bf16)).astype(f32)).astype(bf16)


def across(other_part, own_part):
    chip = chip_sum(other_part, own_part)
    return chip.astype(f32) + swap_x(chip).astype(f32)


def group_route(apart, sources):
    count = lax.axis_size("dp")
    route = []
    for base in range(0, count, GROUP_DEVICES):
        route += [(base + s, base + (s ^ apart)) for s in sources]
    return route

def by_row(*shape):
    return pl.BlockSpec(shape, lambda i, *rest: (i,) + (0,) * (len(shape) - 1))


def at_row(place, *shape):
    return pl.BlockSpec(shape, lambda i, *rest: (place,) + (0,) * (len(shape) - 1))


def whole(*shape):
    return pl.BlockSpec(shape, lambda *at: (0,) * len(shape))


def turned(values, cosine, sine):
    return values * cosine + pltpu.roll(values, values.shape[-1] // 2, 1) * sine


def bring_kernel(columns_ref, core_ref, in_ref, out_ref):
    core = core_ref[0]
    out_ref[:, 0:1] = in_ref[:, pl.ds(core, 1)]
    out_ref[:, 1:2] = in_ref[:, pl.ds(1 - core, 1)]


def place_kernel(columns_ref, core_ref, own_ref, other_ref, out_ref):
    core = core_ref[0]
    out_ref[:, pl.ds(core, 1)] = own_ref[...][:, None]
    out_ref[:, pl.ds(1 - core, 1)] = other_ref[...][:, None]


def heads_kernel(sizes, proj_ref, cos_ref, sin_ref, gain_ref, q_ref, kv_ref, gate_ref):
    query_cols, key_cols, head_dim = sizes
    cosine, sine = cos_ref[...], sin_ref[...]
    for start in range(0, query_cols + key_cols, head_dim):
        values = proj_ref[:, start : start + head_dim]
        gain = gain_ref[0:1] if start < query_cols else gain_ref[1:2]
        low = turned(values * recip_rms(values) * gain, cosine, sine).astype(bf16)
        if start < query_cols:
            q_ref[:, start : start + head_dim] = low
        else:
            kv_ref[:, start - query_cols : start - query_cols + head_dim] = low
    values = proj_ref[:, query_cols + key_cols : query_cols + 2 * key_cols]
    kv_ref[:, key_cols:] = values.astype(bf16)
    gate_ref[...] = jax.nn.sigmoid(proj_ref[:, query_cols + 2 * key_cols :])


def attend_kernel(
    sizes, flag_ref, q_ref, kv_ref, far_ref, col_ref, row_ref, gate_ref, gated_ref, att_ref, lse_ref
):
    head_dim, key_cols, kv_heads, repeat_heads, scale = sizes
    no_far = jnp.where(flag_ref[pl.program_id(0)] == 1, masked, 0.0)
    columns, rows = col_ref[...], row_ref[0]
    own = (columns[:, 0:1] == rows[0:1]) & (rows[1:2] <= columns[:, 1:2])
    for kv_head in range(kv_heads):
        at = slice(kv_head * head_dim, (kv_head + 1) * head_dim)
        at_value = slice(key_cols + kv_head * head_dim, key_cols + (kv_head + 1) * head_dim)
        for head in range(kv_head * repeat_heads, (kv_head + 1) * repeat_heads):
            here = slice(head * head_dim, (head + 1) * head_dim)
            queries = q_ref[:, here]
            far = by_transpose(queries, far_ref[:, at]) * scale + no_far
            near = jnp.where(own, by_transpose(queries, kv_ref[:, at]) * scale, masked)
            peak = jnp.maximum(
                jnp.max(far, axis=-1, keepdims=True), jnp.max(near, axis=-1, keepdims=True)
            )
            far = jnp.exp(far - peak)
            near = jnp.exp(near - peak)
            total = jnp.sum(far, axis=-1, keepdims=True) + jnp.sum(near, axis=-1, keepdims=True)
            share = 1.0 / total
            attended = product((far * share).astype(bf16), far_ref[:, at_value]) + product(
                (near * share).astype(bf16), kv_ref[:, at_value]
            )
            att_ref[:, here] = attended
            gated_ref[:, here] = (attended * gate_ref[:, head : head + 1]).astype(bf16)
            lse_ref[:, head : head + 1] = peak + jnp.log(total)


def attend_back_kernel(
    sizes,
    flag_ref,
    q_ref,
    kv_ref,
    far_ref,
    col_ref,
    row_ref,
    gate_ref,
    att_ref,
    lse_ref,
    grad_ref,
    proj_ref,
    cos_ref,
    sin_ref,
    gain_ref,
    dq_ref,
    dfar_ref,
    dkv_ref,
    logit_ref,
    dgain_ref,
):
    micro, head_dim, key_cols, kv_heads, repeat_heads, scale = sizes
    no_far = jnp.where(flag_ref[micro] == 1, masked, 0.0)
    columns, rows = col_ref[...], row_ref[0]
    own = (columns[:, 0:1] == rows[0:1]) & (rows[1:2] <= columns[:, 1:2])
    cosine, sine, gain = cos_ref[...], sin_ref[...], gain_ref[0:1]
    logit_ref[...] = jnp.zeros_like(logit_ref)
    gain_sum = jnp.zeros((1, head_dim), f32)
    for kv_head in range(kv_heads):
        at = slice(kv_head * head_dim, (kv_head + 1) * head_dim)
        at_value = slice(key_cols + kv_head * head_dim, key_cols + (kv_head + 1) * head_dim)
        totals = [0.0, 0.0, 0.0, 0.0]
        for head in range(kv_head * repeat_heads, (kv_head + 1) * repeat_heads):
            here = slice(head * head_dim, (head + 1) * head_dim)
            queries = q_ref[:, here]
            gate = gate_ref[:, head : head + 1]
            gated_grad, attended = grad_ref[:, here], att_ref[:, here]
            weighted = jnp.sum(gated_grad * attended, axis=-1, keepdims=True)
            logit_ref[:, head : head + 1] = (weighted * gate * (1.0 - gate)).astype(bf16)
            low = (gated_grad * gate).astype(bf16)
            delta = jnp.sum(low.astype(f32) * attended, axis=-1, keepdims=True)
            log_total = lse_ref[:, head : head + 1]
            far = jnp.exp(by_transpose(queries, far_ref[:, at]) * scale + (no_far - log_total))
            near = by_transpose(queries, kv_ref[:, at]) * scale
            near = jnp.exp(jnp.where(own, near - log_total, masked))
            far_low = (far * (by_transpose(low, far_ref[:, at_value]) - delta)).astype(bf16)
            near_low = (near * (by_transpose(low, kv_ref[:, at_value]) - delta)).astype(bf16)
            totals[0] = totals[0] + transpose_by(far_low, queries)
            totals[1] = totals[1] + transpose_by(far.astype(bf16), low)
            totals[2] = totals[2] + transpose_by(near_low, queries)
            totals[3] = totals[3] + transpose_by(near.astype(bf16), low)
            back = (product(far_low, far_ref[:, at]) + product(near_low, kv_ref[:, at])) * scale
            values = proj_ref[:, here]
            back, terms = rms_back(
                values, recip_rms(values), gain, turned(back, cosine, -sine)
            )
            dq_ref[:, here] = back.astype(bf16)
            gain_sum = gain_sum + jnp.sum(terms, axis=0, keepdims=True)
        dfar_ref[:, at] = (totals[0] * scale).astype(bf16)
        dfar_ref[:, at_value] = totals[1].astype(bf16)
        dkv_ref[:, at] = totals[2] * scale
        dkv_ref[:, at_value] = totals[3]
    dgain_ref[...] = jnp.broadcast_to(gain_sum, dgain_ref.shape)


def join_kernel(
    sizes,
    flag_ref,
    dq_ref,
    dkv_ref,
    one_ref,
    two_ref,
    three_ref,
    logit_ref,
    proj_ref,
    cos_ref,
    sin_ref,
    gain_ref,
    out_ref,
    dgain_ref,
):
    micro, query_cols, key_cols, head_dim = sizes
    prompt = flag_ref[micro] == 1
    cosine, sine, gain = cos_ref[...], sin_ref[...], gain_ref[1:2]
    out_ref[:, :query_cols] = dq_ref[...]
    out_ref[:, query_cols + 2 * key_cols :] = logit_ref[...]
    gain_sum = jnp.zeros((1, head_dim), f32)
    for start in range(0, 2 * key_cols, head_dim):
        at = slice(start, start + head_dim)
        arrived = one_ref[:, at].astype(f32) + two_ref[:, at].astype(f32)
        arrived = arrived + three_ref[:, at].astype(f32)
        total = dkv_ref[:, at] + jnp.where(prompt, arrived, 0.0)
        if start < key_cols:
            values = proj_ref[:, at]
            total, terms = rms_back(
                values, recip_rms(values), gain, turned(total, cosine, -sine)
            )
            gain_sum = gain_sum + jnp.sum(terms, axis=0, keepdims=True)
        out_ref[:, query_cols + start : query_cols + start + head_dim] = total.astype(bf16)
    dgain_ref[...] = jnp.broadcast_to(gain_sum, dgain_ref.shape)


def cost(flops, nbytes, exps=0):
    return pl.CostEstimate(flops=flops, bytes_accessed=nbytes, transcendentals=exps)


vmem_bytes = 56 << 20


def on_device(
    tokens,
    cotangent,
    query_weight,
    key_matrix,
    value_matrix,
    head_gate_weight,
    out_weight,
    gate_weight,
    up_weight,
    down_weight,
    norm_attn,
    norm_mlp,
    norm_query,
    norm_key,
    cont_lengths,
):
    count = lax.axis_size("dp")
    dp_index = lax.axis_index("dp")
    core = lax.axis_index("mp") % 2
    place = jnp.where(dp_index % 2 == 0, dp_index // 2, count - 1 - dp_index // 2)
    offset = dp_index % GROUP_DEVICES
    group_index = dp_index // GROUP_DEVICES
    total_rows, width = tokens.shape
    block_rows = total_rows // MICRO_BATCHES
    own_rows = block_rows // 2
    depth = width // count
    head_dim = norm_query.shape[0]
    head_count = head_gate_weight.shape[1]
    query_cols = query_weight.shape[1]
    key_cols = key_matrix.shape[1]
    kv_heads = key_cols // head_dim
    repeat_heads = head_count // kv_heads
    hidden_units = gate_weight.shape[1]
    score_scale = head_dim ** (-0.5)
    gain_query = norm_query.astype(f32)
    key_gain = norm_key.astype(f32)
    first_place = (place + count - (count // 2 - 1)) % count
    places = ring_order(count)

    extra = 128
    lane = lax.broadcasted_iota(jnp.int32, (depth, extra), 1)
    small = jnp.pad(head_gate_weight, ((0, 0), (0, extra - head_count)))
    small = jnp.where(lane == head_count, norm_attn[:, None], small)
    small = jnp.where(lane == head_count + 1, norm_mlp[:, None], small)
    packed = jnp.concatenate([query_weight, key_matrix, value_matrix, small], axis=1)
    in_ring = Gather(jnp.concatenate([packed, out_weight.T], axis=1), count)
    in_ring.issue()

    params = pltpu.CompilerParams(vmem_limit_bytes=vmem_bytes)
    column_places = jnp.asarray(places, jnp.int32)[
        (first_place + jnp.arange(count, dtype=jnp.int32)) % count
    ]
    core_place = core.astype(jnp.int32)[None]

    def rows_in(block):
        halves = block.reshape((MICRO_BATCHES, 2, own_rows) + block.shape[1:])
        swapped = jnp.concatenate([halves[:, 1:], halves[:, :1]], axis=1)
        return jnp.where(core == 0, halves, swapped).reshape(block.shape)

    def bring(block, name):
        if depth % 128:
            ring = [block[:, i * depth : (i + 1) * depth] for i in places]
            block = lax.dynamic_slice_in_dim(
                jnp.concatenate(ring + ring, axis=1), first_place * depth, width, axis=1
            )
            return rows_in(block)
        shape = (MICRO_BATCHES, 2, own_rows, width)
        there = (MICRO_BATCHES, 2, own_rows, depth)
        return pl.pallas_call(
            bring_kernel,
            out_shape=jax.ShapeDtypeStruct(shape, block.dtype),
            grid_spec=pltpu.PrefetchScalarGridSpec(
                num_scalar_prefetch=2,
                grid=(count,),
                in_specs=[pl.BlockSpec(there, lambda i, cols, core: (0, 0, 0, cols[i]))],
                out_specs=pl.BlockSpec(there, lambda i, cols, core: (0, 0, 0, i)),
            ),
            compiler_params=params,
            cost_estimate=cost(0, 2 * block.size * block.dtype.itemsize),
            name=name,
        )(column_places, core_place, block.reshape(shape)).reshape(block.shape)

    def columns_back(block):
        back = lax.dynamic_slice_in_dim(
            jnp.concatenate([block, block], axis=-1),
            ((count - first_place) % count) * depth,
            width,
            axis=-1,
        )
        at = {device: i for i, device in enumerate(places)}
        return jnp.concatenate(
            [back[..., at[i] * depth : (at[i] + 1) * depth] for i in range(count)], axis=-1
        )

    def place_back(own, other, turned, name):
        if depth % 128:
            low = jnp.where(core == 0, own, other)
            high = jnp.where(core == 0, other, own)
            block = jnp.stack([low, high], axis=1).reshape(total_rows, width)
            return columns_back(block) if turned else block
        there = (MICRO_BATCHES, own_rows, depth)
        return pl.pallas_call(
            place_kernel,
            out_shape=jax.ShapeDtypeStruct((MICRO_BATCHES, 2, own_rows, width), own.dtype),
            grid_spec=pltpu.PrefetchScalarGridSpec(
                num_scalar_prefetch=2,
                grid=(count,),
                in_specs=[pl.BlockSpec(there, lambda i, cols, core: (0, 0, i))] * 2,
                out_specs=pl.BlockSpec(
                    (MICRO_BATCHES, 2, own_rows, depth),
                    lambda i, cols, core: (0, 0, 0, cols[i] if turned else i),
                ),
            ),
            compiler_params=params,
            cost_estimate=cost(1024, 1024),
            name=name,
        )(column_places, core_place, own, other).reshape(total_rows, width)

    inputs_low = bring(tokens, "bring_tokens")

    inverse = jnp.power(rope_base, -jnp.arange(head_dim // 2, dtype=f32) * (2.0 / head_dim))
    relatives, segments, positions = [], [], []
    for micro in range(MICRO_BATCHES):
        holder = GROUP_DEVICES - 1 if micro % 2 == 1 else 0
        relative = jnp.bitwise_xor(offset, holder)
        lengths = cont_lengths[group_index, jnp.maximum(relative - 1, 0), micro]
        segment, position = layout(lengths, relative, block_rows)
        relatives.append(relative)
        segments.append(segment)
        positions.append(position)
    segment = rows_in(jnp.concatenate(segments))
    position = rows_in(jnp.concatenate(positions))
    angles = position.astype(f32)[:, None] * inverse[None, :]
    inputs_low, angles = pump(in_ring, inputs_low, angles)
    inputs = inputs_low.astype(f32)
    recip_one = recip_rms(inputs)
    recip_one, cotangent, late_down = pump(in_ring, recip_one, cotangent, down_weight)
    mlp_block = jnp.concatenate([gate_weight, up_weight, late_down.T], axis=1)
    cosine, sine = jnp.cos(angles), jnp.sin(angles)
    cosine = jnp.concatenate([cosine, cosine], axis=1)
    sine = jnp.concatenate([-sine, sine], axis=1)
    spots = jnp.stack([segment, position])
    spot_cols = spots.T
    spot_rows = spots.reshape(2, MICRO_BATCHES, block_rows).transpose(1, 0, 2)
    prompts = jnp.stack([(r == 0).astype(jnp.int32) for r in relatives])
    head_gain = jnp.stack([gain_query, key_gain])

    recip_one, cosine, sine, mlp_block = pump(in_ring, recip_one, cosine, sine, mlp_block)
    recip_one, mlp_block = drain(in_ring, recip_one, mlp_block)
    mlp_ring = Gather(mlp_block, count)
    mlp_ring.issue()
    joined = packed.shape[1]
    in_full = in_ring.gathered(0, joined)
    out_turned = in_ring.gathered(joined, joined + query_cols)
    first_gain = query_cols + 2 * key_cols + head_count
    gain_attn = in_full[:, first_gain].astype(f32)[None, :]
    gain_mlp = in_full[:, first_gain + 1].astype(f32)[None, :]
    normed_one = (inputs * recip_one * gain_attn).astype(bf16)
    projected = product(normed_one, in_full)
    rotated_queries, own_kv, head_gate = pl.pallas_call(
        functools.partial(heads_kernel, (query_cols, key_cols, head_dim)),
        out_shape=(
            jax.ShapeDtypeStruct((total_rows, query_cols), bf16),
            jax.ShapeDtypeStruct((total_rows, 2 * key_cols), bf16),
            jax.ShapeDtypeStruct((total_rows, extra), f32),
        ),
        grid=(total_rows // own_rows,),
        in_specs=[
            by_row(own_rows, joined),
            by_row(own_rows, head_dim),
            by_row(own_rows, head_dim),
            whole(2, head_dim),
        ],
        out_specs=(
            by_row(own_rows, query_cols),
            by_row(own_rows, 2 * key_cols),
            by_row(own_rows, extra),
        ),
        compiler_params=params,
        cost_estimate=cost(total_rows * joined * 20, total_rows * joined * 7),
        name="heads",
    )(projected, cosine, sine, head_gain)

    first_kv, second_kv = own_kv[:block_rows], own_kv[block_rows:]
    sent = jnp.where(offset == 0, first_kv, second_kv)
    by_one = lax.ppermute(sent, "dp", group_route(1, (0, 3)))
    by_two = lax.ppermute(sent, "dp", group_route(2, (0, 3)))
    by_both = lax.ppermute(sent, "dp", group_route(3, (0, 3)))
    far_kv = [
        jnp.where(offset == 1, by_one, jnp.where(offset == 2, by_two, by_both)),
        jnp.where(offset == 2, by_one, jnp.where(offset == 1, by_two, by_both)),
    ]

    far_kv = jnp.concatenate(far_kv, axis=0)
    far_kv, cotangent = pump(mlp_ring, far_kv, cotangent)
    sizes = (head_dim, key_cols, kv_heads, repeat_heads, score_scale)
    pairs = total_rows * 2 * block_rows * query_cols
    gated_all, attended, log_totals = pl.pallas_call(
        functools.partial(attend_kernel, sizes),
        out_shape=(
            jax.ShapeDtypeStruct((total_rows, query_cols), bf16),
            jax.ShapeDtypeStruct((total_rows, query_cols), f32),
            jax.ShapeDtypeStruct((total_rows, extra), f32),
        ),
        grid_spec=pltpu.PrefetchScalarGridSpec(
            num_scalar_prefetch=1,
            grid=(MICRO_BATCHES, 2),
            in_specs=[
                pl.BlockSpec((own_rows, query_cols), lambda m, i, flag: (2 * m + i, 0)),
                pl.BlockSpec((block_rows, 2 * key_cols), lambda m, i, flag: (m, 0)),
                pl.BlockSpec((block_rows, 2 * key_cols), lambda m, i, flag: (m, 0)),
                pl.BlockSpec((own_rows, 2), lambda m, i, flag: (2 * m + i, 0)),
                pl.BlockSpec((1, 2, block_rows), lambda m, i, flag: (m, 0, 0)),
                pl.BlockSpec((own_rows, extra), lambda m, i, flag: (2 * m + i, 0)),
            ],
            out_specs=(
                pl.BlockSpec((own_rows, query_cols), lambda m, i, flag: (2 * m + i, 0)),
                pl.BlockSpec((own_rows, query_cols), lambda m, i, flag: (2 * m + i, 0)),
                pl.BlockSpec((own_rows, extra), lambda m, i, flag: (2 * m + i, 0)),
            ),
        ),
        compiler_params=params,
        cost_estimate=cost(4 * pairs, total_rows * query_cols * 12, pairs // head_dim),
        name="attend",
    )(prompts, rotated_queries, own_kv, far_kv, spot_cols, spot_rows, head_gate)

    gated_all, cotangent = order(gated_all, cotangent)
    upstream_low = bring(cotangent, "bring_cotangent")
    gated_all, upstream_low = pump(mlp_ring, gated_all, upstream_low)
    middles, recips_two, norms_two = [], [], []
    for micro in range(MICRO_BATCHES):
        base = micro * block_rows
        gated_low = gated_all[base : base + block_rows]
        summed = across(
            by_transpose(gated_low[own_rows:], out_turned),
            by_transpose(gated_low[:own_rows], out_turned),
        )
        middle = inputs[base : base + own_rows] + summed
        recip_two = recip_rms(middle)
        own_norm = (middle * recip_two * gain_mlp).astype(bf16)
        if micro == 0:
            own_norm = pump(mlp_ring, own_norm)
        middles.append(middle)
        recips_two.append(recip_two)
        norms_two += [own_norm, swap_core(own_norm)]
    normed_two = jnp.concatenate(norms_two, axis=0)
    normed_two = drain(mlp_ring, normed_two)
    gate_up_full = mlp_ring.gathered(0, 2 * hidden_units)
    down_turned = mlp_ring.gathered(2 * hidden_units, 3 * hidden_units)
    pre = product(normed_two, gate_up_full)
    gate_pre, up_pre = pre[:, :hidden_units], pre[:, hidden_units:]
    sigmoid_gate = jax.nn.sigmoid(gate_pre)
    swish_gate = gate_pre * sigmoid_gate
    hidden_low = (swish_gate * up_pre).astype(bf16)
    down_back = Scatter(
        lambda slot, left=hidden_low, right=upstream_low: transpose_by(
            left, right[:, slot * depth : (slot + 1) * depth]
        ),
        count,
        False,
    )
    (upstream_late,) = down_back.issue(upstream_low)
    hidden_grad = product(upstream_late, down_turned)
    gate_grad = (
        hidden_grad * up_pre * sigmoid_gate * (1.0 + gate_pre * (1.0 - sigmoid_gate))
    ).astype(bf16)
    up_grad = (hidden_grad * swish_gate).astype(bf16)
    gate_grad, up_grad = pump(down_back, gate_grad, up_grad)
    gate_up_grad = jnp.concatenate([gate_grad, up_grad], axis=1)
    partial = by_transpose(gate_up_grad, gate_up_full).astype(bf16)
    partial, gate_up_late = pump(down_back, partial, gate_up_grad)
    gate_up_back = Scatter(
        lambda slot, left=normed_two, right=gate_up_late: transpose_by(
            left[:, slot * depth : (slot + 1) * depth], right
        ),
        count,
    )
    parts = [partial[i * own_rows : (i + 1) * own_rows] for i in range(2 * MICRO_BATCHES)]
    from_other = swap_core(jnp.concatenate(parts[1::2]))
    chips = [
        (parts[2 * i].astype(f32) + from_other[i * own_rows : (i + 1) * own_rows].astype(f32)).astype(
            bf16
        )
        for i in range(MICRO_BATCHES)
    ]
    summed_parts = [part.astype(f32) + swap_x(part).astype(f32) for part in chips]
    (hidden_late,) = gate_up_back.issue(hidden_low)
    hidden_late = pump(down_back, hidden_late)
    parts = [hidden_late[i * own_rows : (i + 1) * own_rows] for i in range(2 * MICRO_BATCHES)]
    mlp_other = by_transpose(jnp.concatenate(parts[1::2]), down_turned).astype(bf16)
    mlp_own = by_transpose(jnp.concatenate(parts[::2]), down_turned).astype(bf16)
    mlp_out = across(mlp_other, mlp_own)

    middle_grads, middle_lows = [], []
    in_grads, query_gain, key_gain_sums, joins, far_grads, kv_grads = [], [], [], [], [], []
    for micro in range(MICRO_BATCHES):
        base = micro * block_rows
        own, other = slice(base, base + own_rows), slice(base + own_rows, base + block_rows)
        summed = summed_parts[micro]
        if micro == 0:
            summed = drain(down_back, summed)
            summed = pump(gate_up_back, summed)
        else:
            kv_grads[0], summed = pump(gate_up_back, kv_grads[0], summed)
        middle_back, _ = rms_back(middles[micro], recips_two[micro], gain_mlp, summed)
        middle_grad = upstream_low[own].astype(f32) + middle_back
        middle_grads.append(middle_grad)
        own_low = middle_grad.astype(bf16)
        middle_lows.append(jnp.concatenate([own_low, swap_core(own_low)], axis=0))
        gated_grad = product(middle_lows[micro], out_turned)
        query_grad, far_grad, kv_grad, logit_grad, query_terms = pl.pallas_call(
            functools.partial(attend_back_kernel, (micro,) + sizes),
            out_shape=(
                jax.ShapeDtypeStruct((block_rows, query_cols), bf16),
                jax.ShapeDtypeStruct((block_rows, 2 * key_cols), bf16),
                jax.ShapeDtypeStruct((block_rows, 2 * key_cols), f32),
                jax.ShapeDtypeStruct((block_rows, extra), bf16),
                jax.ShapeDtypeStruct((8, head_dim), f32),
            ),
            grid_spec=pltpu.PrefetchScalarGridSpec(
                num_scalar_prefetch=1,
                grid=(1,),
                in_specs=[
                    at_row(micro, block_rows, query_cols),
                    at_row(micro, block_rows, 2 * key_cols),
                    at_row(micro, block_rows, 2 * key_cols),
                    at_row(micro, block_rows, 2),
                    at_row(micro, 1, 2, block_rows),
                    at_row(micro, block_rows, extra),
                    at_row(micro, block_rows, query_cols),
                    at_row(micro, block_rows, extra),
                    at_row(0, block_rows, query_cols),
                    at_row(micro, block_rows, query_cols),
                    at_row(micro, block_rows, head_dim),
                    at_row(micro, block_rows, head_dim),
                    whole(2, head_dim),
                ],
                out_specs=(
                    at_row(0, block_rows, query_cols),
                    at_row(0, block_rows, 2 * key_cols),
                    at_row(0, block_rows, 2 * key_cols),
                    at_row(0, block_rows, extra),
                    at_row(0, 8, head_dim),
                ),
            ),
            compiler_params=params,
            cost_estimate=cost(
                5 * pairs, block_rows * query_cols * 30, pairs // head_dim // 2
            ),
            name="attend_back",
        )(
            prompts,
            rotated_queries,
            own_kv,
            far_kv,
            spot_cols,
            spot_rows,
            head_gate,
            attended,
            log_totals,
            gated_grad,
            projected,
            cosine,
            sine,
            head_gain,
        )
        query_gain.append(query_terms[0])
        far_grads.append(far_grad)
        joins.append((query_grad, logit_grad))
        kv_grads.append(kv_grad)
    far_grads[1] = settle(gate_up_back, far_grads[1])
    arrived = [
        lax.ppermute(
            jnp.where(offset == apart, far_grads[0], far_grads[1]),
            "dp",
            group_route(apart, (apart, (GROUP_DEVICES - 1) ^ apart)),
        )
        for apart in (1, 2, 3)
    ]
    mlp_out, kv_grads[1] = order(mlp_out, kv_grads[1])
    layer_own = (jnp.concatenate(middles) + mlp_out).astype(bf16)
    layer_own = layer_own.reshape(MICRO_BATCHES, own_rows, width)
    layer_out = place_back(layer_own, swap_core(layer_own), True, "place_layer")
    layer_out, kv_grads[0] = order(layer_out, kv_grads[0])
    *arrived, kv_grads[0], kv_grads[1] = pump(gate_up_back, *arrived, kv_grads[0], kv_grads[1])
    for micro in range(MICRO_BATCHES):
        query_grad, logit_grad = joins[micro]
        kv_grad = kv_grads[micro]
        in_grad, key_terms = pl.pallas_call(
            functools.partial(join_kernel, (micro, query_cols, key_cols, head_dim)),
            out_shape=(
                jax.ShapeDtypeStruct((block_rows, joined), bf16),
                jax.ShapeDtypeStruct((8, head_dim), f32),
            ),
            grid_spec=pltpu.PrefetchScalarGridSpec(
                num_scalar_prefetch=1,
                grid=(1,),
                in_specs=[
                    at_row(0, block_rows, query_cols),
                    at_row(0, block_rows, 2 * key_cols),
                    at_row(0, block_rows, 2 * key_cols),
                    at_row(0, block_rows, 2 * key_cols),
                    at_row(0, block_rows, 2 * key_cols),
                    at_row(0, block_rows, extra),
                    pl.BlockSpec(
                        (block_rows, key_cols),
                        lambda i, flag, micro=micro: (micro, query_cols // key_cols),
                    ),
                    at_row(micro, block_rows, head_dim),
                    at_row(micro, block_rows, head_dim),
                    whole(2, head_dim),
                ],
                out_specs=(at_row(0, block_rows, joined), at_row(0, 8, head_dim)),
            ),
            compiler_params=params,
            cost_estimate=cost(1024, 1024),
            name="join",
        )(
            prompts,
            query_grad,
            kv_grad,
            *arrived,
            logit_grad,
            projected,
            cosine,
            sine,
            head_gain,
        )
        in_grads.append(in_grad)
        key_gain_sums.append(key_terms[0])
    in_back = Scatter(
        lambda slot, right=jnp.concatenate(in_grads), middle_low=jnp.concatenate(
            middle_lows
        ): jnp.concatenate(
            [
                transpose_by(normed_one[:, slot * depth : (slot + 1) * depth], right),
                transpose_by(middle_low[:, slot * depth : (slot + 1) * depth], gated_all),
            ],
            axis=1,
        ),
        count,
    )
    in_grads = in_back.issue(*in_grads)
    query_gain, key_gain_sum = query_gain[0] + query_gain[1], key_gain_sums[0] + key_gain_sums[1]
    head_gains = jnp.stack([query_gain, key_gain_sum])
    head_gains = head_gains + swap_core(head_gains)
    head_gains = head_gains + swap_x(head_gains)
    first, second, head_gains = settle(gate_up_back, *in_grads, head_gains)
    first = by_transpose(first, in_full).astype(bf16)
    second = by_transpose(second, in_full).astype(bf16)
    chips = [chip_sum(partial[own_rows:], partial[:own_rows]) for partial in (first, second)]
    from_x = [swap_x(chip) for chip in chips]
    chips[1], head_gains = pump(in_back, chips[1], head_gains)
    level, turn = 1, 0
    while level < count // 2:
        arrived_gains, from_x[turn] = pump(in_back, swap_dp(head_gains, level), from_x[turn])
        head_gains = head_gains + arrived_gains
        level, turn = 2 * level, min(turn + 1, MICRO_BATCHES - 1)
    input_rows = []
    for micro in range(MICRO_BATCHES):
        own = slice(micro * block_rows, micro * block_rows + own_rows)
        summed = chips[micro].astype(f32) + from_x[micro].astype(f32)
        input_back, _ = rms_back(inputs[own], recip_one[own], gain_attn, summed)
        input_rows.append(middle_grads[micro] + input_back)
    input_own = jnp.stack(input_rows)
    tokens_grad = place_back(input_own, swap_core(input_own), True, "place_tokens")

    arrived_gains, tokens_grad = pump(in_back, swap_dp(head_gains, level), tokens_grad)
    head_gains = head_gains + arrived_gains
    tokens_grad = drain(in_back, tokens_grad)
    drain(gate_up_back)

    gate_up_grad = gate_up_back.total()
    in_total = in_back.total()
    in_weight_grad, out_weight_grad = in_total[:, :joined], in_total[:, joined:].T
    mlp_sum = jnp.sum(
        gate_up_grad[:, :hidden_units] * gate_weight.astype(f32)
        + gate_up_grad[:, hidden_units:] * up_weight.astype(f32),
        axis=1,
    )
    used = first_gain
    attn_sum = jnp.sum(in_weight_grad[:, :used] * packed[:, :used].astype(f32), axis=1)
    gains = jnp.stack([attn_sum, mlp_sum])
    for swap in (swap_core, swap_x):
        gains = gains + swap(gains)
    return (
        layer_out,
        tokens_grad,
        in_weight_grad[:, :query_cols],
        in_weight_grad[:, query_cols : query_cols + key_cols],
        in_weight_grad[:, query_cols + key_cols : query_cols + 2 * key_cols],
        in_weight_grad[:, query_cols + 2 * key_cols : query_cols + 2 * key_cols + head_count],
        out_weight_grad,
        gate_up_grad[:, :hidden_units],
        gate_up_grad[:, hidden_units:],
        down_back.total(),
        gains[0] / norm_attn.astype(f32),
        gains[1] / norm_mlp.astype(f32),
        head_gains[0],
        head_gains[1],
    )


def solution(mesh):
    rows, weight, turned = P("dp", None), P("dp", "mp"), P("mp", "dp")
    weights = (weight, weight, weight, weight, turned, weight, weight, turned)
    placed = (rows, rows) + weights + (P("dp"), P("dp"), P(), P())
    return jax.shard_map(
        on_device, mesh=mesh, in_specs=placed + (P(),), out_specs=placed, check_vma=False
    )
```

```python
import functools

import jax
import jax.numpy as jnp
from jax import lax
from jax.experimental import pallas as pl
from jax.experimental.pallas import tpu as pltpu
from jax.sharding import PartitionSpec as P

MICRO_BATCHES = 2
GROUP_DEVICES = 4

eps = 1e-06
rope_base = 1000000.0
masked = -1e30
f32 = jnp.float32
bf16 = jnp.bfloat16


def product(left_side, right_side):
    return jnp.dot(left_side, right_side, preferred_element_type=f32)


def by_transpose(left_side, right_side):
    return lax.dot_general(
        left_side, right_side, (((1,), (1,)), ((), ())), preferred_element_type=f32
    )


def transpose_by(left_side, right_side):
    return lax.dot_general(
        left_side, right_side, (((0,), (0,)), ((), ())), preferred_element_type=f32
    )


def recip_rms(values):
    return lax.rsqrt(jnp.mean(values * values, axis=-1, keepdims=True) + eps)


def rms_back(values, reciprocal, gain, gradient):
    scaled = gain * gradient
    cubed = reciprocal * reciprocal * reciprocal
    back = reciprocal * scaled - values * cubed * jnp.mean(scaled * values, axis=-1, keepdims=True)
    return (back, gradient * values * reciprocal)


def layout(lengths, relative, row_count):
    seg_ends = jnp.cumsum(lengths, dtype=jnp.int32)
    starts = seg_ends - lengths
    row_ids = jnp.arange(row_count, dtype=jnp.int32)
    seg_index = jnp.sum(
        (row_ids[:, None] >= seg_ends[None, :]).astype(jnp.int32), axis=1, dtype=jnp.int32
    )
    seg_onehot = seg_index[:, None] == jnp.arange(lengths.shape[0], dtype=jnp.int32)[None, :]
    seg_start = jnp.sum(jnp.where(seg_onehot, starts[None, :], 0), axis=1, dtype=jnp.int32)
    prompt = relative == 0
    segment = jnp.where(prompt, 0, 1 + seg_index)
    position = jnp.where(prompt, row_ids, row_count + row_ids - seg_start)
    return (segment, position)


def ring_order(count):
    return list(range(0, count, 2)) + list(range(count - 1, 0, -2))


def ring_step(block, count, forward):
    places = ring_order(count)
    turn = 1 if forward else -1
    route = [(places[i], places[(i + turn) % count]) for i in range(count)]
    return lax.ppermute(block, "dp", route)


class Gather:
    def __init__(self, block, count):
        self.count = count
        self.left = count // 2
        self.cut = (block.shape[1] // 256) * 128
        self.held = [[block], [block]]
        self.flying = []

    def issue(self):
        if self.left:
            self.left -= 1
            ahead, behind = self.held[0][-1], self.held[1][-1]
            if not self.left:
                ahead, behind = ahead[:, : self.cut], behind[:, self.cut :]
            self.flying = [
                (0, ring_step(ahead, self.count, True)),
                (1, ring_step(behind, self.count, False)),
            ]

    def land(self, arrays):
        for (way, _), array in zip(self.flying, arrays):
            self.held[way].append(array)
        self.flying = []

    def gathered(self, first, end):
        ahead, behind = self.held
        half = self.count // 2
        near = [ahead[step] for step in range(half - 1, -1, -1)]
        near += [behind[step] for step in range(1, half)]
        near.append(jnp.concatenate([ahead[half], behind[half]], axis=1))
        return jnp.concatenate([block[:, first:end] for block in near], axis=0)


class Scatter:
    def __init__(self, chunk, count, split=True):
        half = count // 2
        self.count, self.chunk, self.split = count, chunk, split
        self.own = half - 1
        self.left = half
        self.got = [None, None]
        self.flying = []

    def issue(self, *values):
        parts = []
        if self.left == self.count // 2:
            far = self.chunk(self.own + self.left).astype(bf16)
            cut = far.shape[1] // 256 * 128 or far.shape[1] // 2
            if self.split:
                parts = [(0, far[:, :cut]), (1, far[:, cut:])]
            else:
                ahead = self.chunk(self.own + self.left - 1).astype(bf16)
                parts = [(0, ahead), (1, far)]
        elif self.left > 0:
            late = 0 if self.split else 1
            for way, slot in ((0, self.own + self.left - late), (1, self.own - self.left)):
                if slot == self.own:
                    self.kept = self.got[way]
                    continue
                part, got = self.chunk(slot), self.got[way].astype(f32)
                lack = part.shape[1] - got.shape[1]
                if lack:
                    got = jnp.pad(got, ((0, 0), ((0, lack), (lack, 0))[way]))
                parts.append((way, (part + got).astype(bf16)))
        self.left -= 1
        if parts and values:
            tied = lax.optimization_barrier(tuple(part for _, part in parts) + values)
            parts = [(way, part) for (way, _), part in zip(parts, tied)]
            values = tied[len(parts) :]
        self.flying = [(way, ring_step(part, self.count, way == 0)) for way, part in parts]
        return values

    def land(self, arrays):
        for (way, _), array in zip(self.flying, arrays):
            self.got[way] = array
        self.flying = []

    def total(self):
        if not self.split:
            self.got[0] = self.kept
        return self.chunk(self.own) + self.got[0].astype(f32) + self.got[1].astype(f32)


def single(values):
    return values[0] if len(values) == 1 else values


def pump(ring, *values):
    arrays = [array for _, array in ring.flying]
    if arrays and values:
        tied = lax.optimization_barrier(tuple(arrays) + values)
        arrays, values = list(tied[: len(arrays)]), tied[len(arrays) :]
    ring.land(arrays)
    if isinstance(ring, Scatter):
        values = ring.issue(*values)
    else:
        ring.issue()
    return single(values)


def settle(ring, *values):
    arrays = [array for _, array in ring.flying]
    tied = lax.optimization_barrier(tuple(arrays) + values)
    ring.land(list(tied[: len(arrays)]))
    return single(tied[len(arrays) :])


def drain(ring, *values):
    while ring.flying or ring.left > 0:
        values = pump(ring, *values)
        values = values if isinstance(values, tuple) else (values,)
    return single(values)


def order(*values):
    return lax.optimization_barrier(values)


def swap_core(block):
    return lax.ppermute(block, "mp", [(i, i ^ 1) for i in range(lax.axis_size("mp"))])


def swap_x(block):
    return lax.ppermute(block, "mp", [(i, i ^ 2) for i in range(lax.axis_size("mp"))])


def swap_dp(block, level):
    count = lax.axis_size("dp")
    return lax.ppermute(block, "dp", [(i, i ^ level) for i in range(count)])


def chip_sum(other_part, own_part):
    return (own_part + swap_core(other_part.astype(bf16)).astype(f32)).astype(bf16)


def across(other_part, own_part):
    chip = chip_sum(other_part, own_part)
    return chip.astype(f32) + swap_x(chip).astype(f32)


def group_route(apart, sources):
    count = lax.axis_size("dp")
    route = []
    for base in range(0, count, GROUP_DEVICES):
        route += [(base + s, base + (s ^ apart)) for s in sources]
    return route

def by_row(*shape):
    return pl.BlockSpec(shape, lambda i, *rest: (i,) + (0,) * (len(shape) - 1))


def at_row(place, *shape):
    return pl.BlockSpec(shape, lambda i, *rest: (place,) + (0,) * (len(shape) - 1))


def whole(*shape):
    return pl.BlockSpec(shape, lambda *at: (0,) * len(shape))


def turned(values, cosine, sine):
    return values * cosine + pltpu.roll(values, values.shape[-1] // 2, 1) * sine


def bring_kernel(columns_ref, core_ref, in_ref, out_ref):
    core = core_ref[0]
    out_ref[:, 0:1] = in_ref[:, pl.ds(core, 1)]
    out_ref[:, 1:2] = in_ref[:, pl.ds(1 - core, 1)]


def place_kernel(columns_ref, core_ref, own_ref, other_ref, out_ref):
    core = core_ref[0]
    out_ref[:, pl.ds(core, 1)] = own_ref[...][:, None]
    out_ref[:, pl.ds(1 - core, 1)] = other_ref[...][:, None]


def place_rows_kernel(columns_ref, core_ref, *refs):
    core, out_ref = core_ref[0], refs[-1]
    for micro in range(MICRO_BATCHES):
        out_ref[micro, pl.ds(core, 1)] = refs[micro][...][None]
        out_ref[micro, pl.ds(1 - core, 1)] = refs[MICRO_BATCHES + micro][...][None]


def input_back_kernel(input_ref, chip_ref, other_ref, gain_ref, base_ref, out_ref):
    values = input_ref[...].astype(f32)
    gradient = chip_ref[...].astype(f32) + other_ref[...].astype(f32)
    back, _ = rms_back(values, recip_rms(values), gain_ref[...], gradient)
    out_ref[...] = base_ref[...] + back


def heads_kernel(sizes, proj_ref, cos_ref, sin_ref, gain_ref, q_ref, kv_ref, gate_ref):
    query_cols, key_cols, head_dim = sizes
    cosine, sine = cos_ref[...], sin_ref[...]
    for start in range(0, query_cols + key_cols, head_dim):
        values = proj_ref[:, start : start + head_dim]
        gain = gain_ref[0:1] if start < query_cols else gain_ref[1:2]
        low = turned(values * recip_rms(values) * gain, cosine, sine).astype(bf16)
        if start < query_cols:
            q_ref[:, start : start + head_dim] = low
        else:
            kv_ref[:, start - query_cols : start - query_cols + head_dim] = low
    values = proj_ref[:, query_cols + key_cols : query_cols + 2 * key_cols]
    kv_ref[:, key_cols:] = values.astype(bf16)
    gate_ref[...] = jax.nn.sigmoid(proj_ref[:, query_cols + 2 * key_cols :])


def attend_kernel(
    sizes, flag_ref, q_ref, kv_ref, far_ref, col_ref, row_ref, gate_ref, gated_ref, att_ref, lse_ref
):
    head_dim, key_cols, kv_heads, repeat_heads, scale = sizes
    no_far = jnp.where(flag_ref[pl.program_id(0)] == 1, masked, 0.0)
    columns, rows = col_ref[...], row_ref[0]
    own = (columns[:, 0:1] == rows[0:1]) & (rows[1:2] <= columns[:, 1:2])
    for kv_head in range(kv_heads):
        at = slice(kv_head * head_dim, (kv_head + 1) * head_dim)
        at_value = slice(key_cols + kv_head * head_dim, key_cols + (kv_head + 1) * head_dim)
        for head in range(kv_head * repeat_heads, (kv_head + 1) * repeat_heads):
            here = slice(head * head_dim, (head + 1) * head_dim)
            queries = q_ref[:, here]
            far = by_transpose(queries, far_ref[:, at]) * scale + no_far
            near = jnp.where(own, by_transpose(queries, kv_ref[:, at]) * scale, masked)
            peak = jnp.maximum(
                jnp.max(far, axis=-1, keepdims=True), jnp.max(near, axis=-1, keepdims=True)
            )
            far = jnp.exp(far - peak)
            near = jnp.exp(near - peak)
            total = jnp.sum(far, axis=-1, keepdims=True) + jnp.sum(near, axis=-1, keepdims=True)
            share = 1.0 / total
            attended = product((far * share).astype(bf16), far_ref[:, at_value]) + product(
                (near * share).astype(bf16), kv_ref[:, at_value]
            )
            att_ref[:, here] = attended
            gated_ref[:, here] = (attended * gate_ref[:, head : head + 1]).astype(bf16)
            lse_ref[:, head : head + 1] = peak + jnp.log(total)


def attend_back_kernel(
    sizes,
    flag_ref,
    q_ref,
    kv_ref,
    far_ref,
    col_ref,
    row_ref,
    gate_ref,
    att_ref,
    lse_ref,
    grad_ref,
    proj_ref,
    cos_ref,
    sin_ref,
    gain_ref,
    dq_ref,
    dfar_ref,
    dkv_ref,
    logit_ref,
    dgain_ref,
):
    micro, head_dim, key_cols, kv_heads, repeat_heads, scale = sizes
    no_far = jnp.where(flag_ref[micro] == 1, masked, 0.0)
    columns, rows = col_ref[...], row_ref[0]
    own = (columns[:, 0:1] == rows[0:1]) & (columns[:, 1:2] <= rows[1:2])
    cosine, sine, gain = cos_ref[...], sin_ref[...], gain_ref[0:1]
    logit_ref[...] = jnp.zeros_like(logit_ref)
    lane = lax.broadcasted_iota(jnp.int32, lse_ref.shape, 1)
    deltas = jnp.zeros(lse_ref.shape, f32)
    lows = []
    for head in range(kv_heads * repeat_heads):
        here = slice(head * head_dim, (head + 1) * head_dim)
        gate = gate_ref[:, head : head + 1]
        gated_grad, attended = grad_ref[:, here], att_ref[:, here]
        weighted = jnp.sum(gated_grad * attended, axis=-1, keepdims=True)
        logit_ref[:, head : head + 1] = (weighted * gate * (1.0 - gate)).astype(bf16)
        low = (gated_grad * gate).astype(bf16)
        delta = jnp.sum(low.astype(f32) * attended, axis=-1, keepdims=True)
        deltas = jnp.where(lane == head, delta, deltas)
        lows.append(low)
    deltas, totals_log = deltas.T, lse_ref[...].T
    gain_sum = jnp.zeros((1, head_dim), f32)
    for kv_head in range(kv_heads):
        at = slice(kv_head * head_dim, (kv_head + 1) * head_dim)
        at_value = slice(key_cols + kv_head * head_dim, key_cols + (kv_head + 1) * head_dim)
        totals = [0.0, 0.0, 0.0, 0.0]
        for head in range(kv_head * repeat_heads, (kv_head + 1) * repeat_heads):
            here = slice(head * head_dim, (head + 1) * head_dim)
            queries, low = q_ref[:, here], lows[head]
            delta, log_total = deltas[head : head + 1], totals_log[head : head + 1]
            far = jnp.exp(by_transpose(far_ref[:, at], queries) * scale + (no_far - log_total))
            near = by_transpose(kv_ref[:, at], queries) * scale
            near = jnp.exp(jnp.where(own, near - log_total, masked))
            far_low = (far * (by_transpose(far_ref[:, at_value], low) - delta)).astype(bf16)
            near_low = (near * (by_transpose(kv_ref[:, at_value], low) - delta)).astype(bf16)
            totals[0] = totals[0] + product(far_low, queries)
            totals[1] = totals[1] + product(far.astype(bf16), low)
            totals[2] = totals[2] + product(near_low, queries)
            totals[3] = totals[3] + product(near.astype(bf16), low)
            back = transpose_by(far_low, far_ref[:, at]) + transpose_by(near_low, kv_ref[:, at])
            back = back * scale
            values = proj_ref[:, here]
            back, terms = rms_back(
                values, recip_rms(values), gain, turned(back, cosine, -sine)
            )
            dq_ref[:, here] = back.astype(bf16)
            gain_sum = gain_sum + jnp.sum(terms, axis=0, keepdims=True)
        dfar_ref[:, at] = (totals[0] * scale).astype(bf16)
        dfar_ref[:, at_value] = totals[1].astype(bf16)
        dkv_ref[:, at] = totals[2] * scale
        dkv_ref[:, at_value] = totals[3]
    dgain_ref[...] = jnp.broadcast_to(gain_sum, dgain_ref.shape)


def join_kernel(
    sizes,
    flag_ref,
    dq_ref,
    dkv_ref,
    one_ref,
    two_ref,
    three_ref,
    logit_ref,
    proj_ref,
    cos_ref,
    sin_ref,
    gain_ref,
    out_ref,
    dgain_ref,
):
    micro, query_cols, key_cols, head_dim = sizes
    prompt = flag_ref[micro] == 1
    cosine, sine, gain = cos_ref[...], sin_ref[...], gain_ref[1:2]
    out_ref[:, :query_cols] = dq_ref[...]
    out_ref[:, query_cols + 2 * key_cols :] = logit_ref[...]
    gain_sum = jnp.zeros((1, head_dim), f32)
    for start in range(0, 2 * key_cols, head_dim):
        at = slice(start, start + head_dim)
        arrived = one_ref[:, at].astype(f32) + two_ref[:, at].astype(f32)
        arrived = arrived + three_ref[:, at].astype(f32)
        total = dkv_ref[:, at] + jnp.where(prompt, arrived, 0.0)
        if start < key_cols:
            values = proj_ref[:, at]
            total, terms = rms_back(
                values, recip_rms(values), gain, turned(total, cosine, -sine)
            )
            gain_sum = gain_sum + jnp.sum(terms, axis=0, keepdims=True)
        out_ref[:, query_cols + start : query_cols + start + head_dim] = total.astype(bf16)
    dgain_ref[...] = jnp.broadcast_to(gain_sum, dgain_ref.shape)


def cost(flops, nbytes, exps=0):
    return pl.CostEstimate(flops=flops, bytes_accessed=nbytes, transcendentals=exps)


vmem_bytes = 56 << 20


def on_device(
    tokens,
    cotangent,
    query_weight,
    key_matrix,
    value_matrix,
    head_gate_weight,
    out_weight,
    gate_weight,
    up_weight,
    down_weight,
    norm_attn,
    norm_mlp,
    norm_query,
    norm_key,
    cont_lengths,
):
    count = lax.axis_size("dp")
    dp_index = lax.axis_index("dp")
    core = lax.axis_index("mp") % 2
    place = jnp.where(dp_index % 2 == 0, dp_index // 2, count - 1 - dp_index // 2)
    offset = dp_index % GROUP_DEVICES
    group_index = dp_index // GROUP_DEVICES
    total_rows, width = tokens.shape
    block_rows = total_rows // MICRO_BATCHES
    own_rows = block_rows // 2
    depth = width // count
    head_dim = norm_query.shape[0]
    head_count = head_gate_weight.shape[1]
    query_cols = query_weight.shape[1]
    key_cols = key_matrix.shape[1]
    kv_heads = key_cols // head_dim
    repeat_heads = head_count // kv_heads
    hidden_units = gate_weight.shape[1]
    score_scale = head_dim ** (-0.5)
    gain_query = norm_query.astype(f32)
    key_gain = norm_key.astype(f32)
    first_place = (place + count - (count // 2 - 1)) % count
    places = ring_order(count)

    extra = 128
    lane = lax.broadcasted_iota(jnp.int32, (depth, extra), 1)
    small = jnp.pad(head_gate_weight, ((0, 0), (0, extra - head_count)))
    small = jnp.where(lane == head_count, norm_attn[:, None], small)
    small = jnp.where(lane == head_count + 1, norm_mlp[:, None], small)
    packed = jnp.concatenate([query_weight, key_matrix, value_matrix, small], axis=1)
    in_ring = Gather(jnp.concatenate([packed, out_weight.T], axis=1), count)
    in_ring.issue()

    params = pltpu.CompilerParams(vmem_limit_bytes=vmem_bytes)
    column_places = jnp.asarray(places, jnp.int32)[
        (first_place + jnp.arange(count, dtype=jnp.int32)) % count
    ]
    core_place = core.astype(jnp.int32)[None]

    def rows_in(block):
        halves = block.reshape((MICRO_BATCHES, 2, own_rows) + block.shape[1:])
        swapped = jnp.concatenate([halves[:, 1:], halves[:, :1]], axis=1)
        return jnp.where(core == 0, halves, swapped).reshape(block.shape)

    def bring(block, name):
        if depth % 128:
            ring = [block[:, i * depth : (i + 1) * depth] for i in places]
            block = lax.dynamic_slice_in_dim(
                jnp.concatenate(ring + ring, axis=1), first_place * depth, width, axis=1
            )
            return rows_in(block)
        shape = (MICRO_BATCHES, 2, own_rows, width)
        there = (MICRO_BATCHES, 2, own_rows, depth)
        return pl.pallas_call(
            bring_kernel,
            out_shape=jax.ShapeDtypeStruct(shape, block.dtype),
            grid_spec=pltpu.PrefetchScalarGridSpec(
                num_scalar_prefetch=2,
                grid=(count,),
                in_specs=[pl.BlockSpec(there, lambda i, cols, core: (0, 0, 0, cols[i]))],
                out_specs=pl.BlockSpec(there, lambda i, cols, core: (0, 0, 0, i)),
            ),
            compiler_params=params,
            cost_estimate=cost(0, 2 * block.size * block.dtype.itemsize),
            name=name,
        )(column_places, core_place, block.reshape(shape)).reshape(block.shape)

    def columns_back(block):
        back = lax.dynamic_slice_in_dim(
            jnp.concatenate([block, block], axis=-1),
            ((count - first_place) % count) * depth,
            width,
            axis=-1,
        )
        at = {device: i for i, device in enumerate(places)}
        return jnp.concatenate(
            [back[..., at[i] * depth : (at[i] + 1) * depth] for i in range(count)], axis=-1
        )

    def place_back(own, other, turned, name):
        if depth % 128:
            low = jnp.where(core == 0, own, other)
            high = jnp.where(core == 0, other, own)
            block = jnp.stack([low, high], axis=1).reshape(total_rows, width)
            return columns_back(block) if turned else block
        there = (MICRO_BATCHES, own_rows, depth)
        return pl.pallas_call(
            place_kernel,
            out_shape=jax.ShapeDtypeStruct((MICRO_BATCHES, 2, own_rows, width), own.dtype),
            grid_spec=pltpu.PrefetchScalarGridSpec(
                num_scalar_prefetch=2,
                grid=(count,),
                in_specs=[pl.BlockSpec(there, lambda i, cols, core: (0, 0, i))] * 2,
                out_specs=pl.BlockSpec(
                    (MICRO_BATCHES, 2, own_rows, depth),
                    lambda i, cols, core: (0, 0, 0, cols[i] if turned else i),
                ),
            ),
            compiler_params=params,
            cost_estimate=cost(1024, 1024),
            name=name,
        )(column_places, core_place, own, other).reshape(total_rows, width)

    inputs_low = bring(tokens, "bring_tokens")

    inverse = jnp.power(rope_base, -jnp.arange(head_dim // 2, dtype=f32) * (2.0 / head_dim))
    relatives, segments, positions = [], [], []
    for micro in range(MICRO_BATCHES):
        holder = GROUP_DEVICES - 1 if micro % 2 == 1 else 0
        relative = jnp.bitwise_xor(offset, holder)
        lengths = cont_lengths[group_index, jnp.maximum(relative - 1, 0), micro]
        segment, position = layout(lengths, relative, block_rows)
        relatives.append(relative)
        segments.append(segment)
        positions.append(position)
    segment = rows_in(jnp.concatenate(segments))
    position = rows_in(jnp.concatenate(positions))
    angles = position.astype(f32)[:, None] * inverse[None, :]
    inputs_low, angles = pump(in_ring, inputs_low, angles)
    inputs = inputs_low.astype(f32)
    recip_one = recip_rms(inputs)
    recip_one, cotangent, late_down = pump(in_ring, recip_one, cotangent, down_weight)
    mlp_block = jnp.concatenate([gate_weight, up_weight, late_down.T], axis=1)
    cosine, sine = jnp.cos(angles), jnp.sin(angles)
    cosine = jnp.concatenate([cosine, cosine], axis=1)
    sine = jnp.concatenate([-sine, sine], axis=1)
    spots = jnp.stack([segment, position])
    spot_cols = spots.T
    spot_rows = spots.reshape(2, MICRO_BATCHES, block_rows).transpose(1, 0, 2)
    prompts = jnp.stack([(r == 0).astype(jnp.int32) for r in relatives])
    head_gain = jnp.stack([gain_query, key_gain])

    recip_one, cosine, sine, mlp_block = pump(in_ring, recip_one, cosine, sine, mlp_block)
    recip_one, mlp_block = drain(in_ring, recip_one, mlp_block)
    mlp_ring = Gather(mlp_block, count)
    mlp_ring.issue()
    joined = packed.shape[1]
    in_full = in_ring.gathered(0, joined)
    out_turned = in_ring.gathered(joined, joined + query_cols)
    first_gain = query_cols + 2 * key_cols + head_count
    gain_attn = in_full[:, first_gain].astype(f32)[None, :]
    gain_mlp = in_full[:, first_gain + 1].astype(f32)[None, :]
    normed_one = (inputs * recip_one * gain_attn).astype(bf16)
    projected = product(normed_one, in_full)
    rotated_queries, own_kv, head_gate = pl.pallas_call(
        functools.partial(heads_kernel, (query_cols, key_cols, head_dim)),
        out_shape=(
            jax.ShapeDtypeStruct((total_rows, query_cols), bf16),
            jax.ShapeDtypeStruct((total_rows, 2 * key_cols), bf16),
            jax.ShapeDtypeStruct((total_rows, extra), f32),
        ),
        grid=(total_rows // own_rows,),
        in_specs=[
            by_row(own_rows, joined),
            by_row(own_rows, head_dim),
            by_row(own_rows, head_dim),
            whole(2, head_dim),
        ],
        out_specs=(
            by_row(own_rows, query_cols),
            by_row(own_rows, 2 * key_cols),
            by_row(own_rows, extra),
        ),
        compiler_params=params,
        cost_estimate=cost(total_rows * joined * 20, total_rows * joined * 7),
        name="heads",
    )(projected, cosine, sine, head_gain)

    first_kv, second_kv = own_kv[:block_rows], own_kv[block_rows:]
    sent = jnp.where(offset == 0, first_kv, second_kv)
    by_one = lax.ppermute(sent, "dp", group_route(1, (0, 3)))
    by_two = lax.ppermute(sent, "dp", group_route(2, (0, 3)))
    by_both = lax.ppermute(sent, "dp", group_route(3, (0, 3)))
    far_kv = [
        jnp.where(offset == 1, by_one, jnp.where(offset == 2, by_two, by_both)),
        jnp.where(offset == 2, by_one, jnp.where(offset == 1, by_two, by_both)),
    ]

    far_kv = jnp.concatenate(far_kv, axis=0)
    far_kv, cotangent = pump(mlp_ring, far_kv, cotangent)
    sizes = (head_dim, key_cols, kv_heads, repeat_heads, score_scale)
    pairs = total_rows * 2 * block_rows * query_cols
    gated_all, attended, log_totals = pl.pallas_call(
        functools.partial(attend_kernel, sizes),
        out_shape=(
            jax.ShapeDtypeStruct((total_rows, query_cols), bf16),
            jax.ShapeDtypeStruct((total_rows, query_cols), f32),
            jax.ShapeDtypeStruct((total_rows, extra), f32),
        ),
        grid_spec=pltpu.PrefetchScalarGridSpec(
            num_scalar_prefetch=1,
            grid=(MICRO_BATCHES, 2),
            in_specs=[
                pl.BlockSpec((own_rows, query_cols), lambda m, i, flag: (2 * m + i, 0)),
                pl.BlockSpec((block_rows, 2 * key_cols), lambda m, i, flag: (m, 0)),
                pl.BlockSpec((block_rows, 2 * key_cols), lambda m, i, flag: (m, 0)),
                pl.BlockSpec((own_rows, 2), lambda m, i, flag: (2 * m + i, 0)),
                pl.BlockSpec((1, 2, block_rows), lambda m, i, flag: (m, 0, 0)),
                pl.BlockSpec((own_rows, extra), lambda m, i, flag: (2 * m + i, 0)),
            ],
            out_specs=(
                pl.BlockSpec((own_rows, query_cols), lambda m, i, flag: (2 * m + i, 0)),
                pl.BlockSpec((own_rows, query_cols), lambda m, i, flag: (2 * m + i, 0)),
                pl.BlockSpec((own_rows, extra), lambda m, i, flag: (2 * m + i, 0)),
            ),
        ),
        compiler_params=params,
        cost_estimate=cost(4 * pairs, total_rows * query_cols * 12, pairs // head_dim),
        name="attend",
    )(prompts, rotated_queries, own_kv, far_kv, spot_cols, spot_rows, head_gate)

    gated_all, cotangent = order(gated_all, cotangent)
    upstream_low = bring(cotangent, "bring_cotangent")
    gated_all, upstream_low = pump(mlp_ring, gated_all, upstream_low)
    middles, recips_two, norms_two = [], [], []
    for micro in range(MICRO_BATCHES):
        base = micro * block_rows
        gated_low = gated_all[base : base + block_rows]
        summed = across(
            by_transpose(gated_low[own_rows:], out_turned),
            by_transpose(gated_low[:own_rows], out_turned),
        )
        middle = inputs[base : base + own_rows] + summed
        recip_two = recip_rms(middle)
        own_norm = (middle * recip_two * gain_mlp).astype(bf16)
        if micro == 0:
            own_norm = pump(mlp_ring, own_norm)
        middles.append(middle)
        recips_two.append(recip_two)
        norms_two += [own_norm, swap_core(own_norm)]
    normed_two = jnp.concatenate(norms_two, axis=0)
    normed_two = drain(mlp_ring, normed_two)
    gate_up_full = mlp_ring.gathered(0, 2 * hidden_units)
    down_turned = mlp_ring.gathered(2 * hidden_units, 3 * hidden_units)
    pre = product(normed_two, gate_up_full).astype(bf16)
    gate_pre, up_pre = pre[:, :hidden_units].astype(f32), pre[:, hidden_units:].astype(f32)
    sigmoid_gate = jax.nn.sigmoid(gate_pre)
    swish_gate = gate_pre * sigmoid_gate
    hidden_low = (swish_gate * up_pre).astype(bf16)
    down_back = Scatter(
        lambda slot, left=hidden_low, right=upstream_low: transpose_by(
            left, right[:, slot * depth : (slot + 1) * depth]
        ),
        count,
        False,
    )
    (upstream_late,) = down_back.issue(upstream_low)
    hidden_grad = product(upstream_late, down_turned)
    gate_grad = (
        hidden_grad * up_pre * sigmoid_gate * (1.0 + gate_pre * (1.0 - sigmoid_gate))
    ).astype(bf16)
    up_grad = (hidden_grad * swish_gate).astype(bf16)
    gate_grad, up_grad = pump(down_back, gate_grad, up_grad)
    gate_up_grad = jnp.concatenate([gate_grad, up_grad], axis=1)
    partial = by_transpose(gate_up_grad, gate_up_full).astype(bf16)
    partial, gate_up_late = pump(down_back, partial, gate_up_grad)
    gate_up_back = Scatter(
        lambda slot, left=normed_two, right=gate_up_late: transpose_by(
            left[:, slot * depth : (slot + 1) * depth], right
        ),
        count,
    )
    parts = [partial[i * own_rows : (i + 1) * own_rows] for i in range(2 * MICRO_BATCHES)]
    from_other = swap_core(jnp.concatenate(parts[1::2]))
    chips = [
        (parts[2 * i].astype(f32) + from_other[i * own_rows : (i + 1) * own_rows].astype(f32)).astype(
            bf16
        )
        for i in range(MICRO_BATCHES)
    ]
    summed_parts = [part.astype(f32) + swap_x(part).astype(f32) for part in chips]
    (hidden_late,) = gate_up_back.issue(hidden_low)
    hidden_late = pump(down_back, hidden_late)
    parts = [hidden_late[i * own_rows : (i + 1) * own_rows] for i in range(2 * MICRO_BATCHES)]
    mlp_other = by_transpose(jnp.concatenate(parts[1::2]), down_turned).astype(bf16)
    mlp_own = by_transpose(jnp.concatenate(parts[::2]), down_turned).astype(bf16)
    mlp_out = across(mlp_other, mlp_own)

    middle_grads, middle_lows = [], []
    in_grads, query_gain, key_gain_sums, joins, far_grads, kv_grads = [], [], [], [], [], []
    for micro in range(MICRO_BATCHES):
        base = micro * block_rows
        own, other = slice(base, base + own_rows), slice(base + own_rows, base + block_rows)
        summed = summed_parts[micro]
        if micro == 0:
            summed = drain(down_back, summed)
            summed = pump(gate_up_back, summed)
        else:
            kv_grads[0], summed = pump(gate_up_back, kv_grads[0], summed)
        middle_back, _ = rms_back(middles[micro], recips_two[micro], gain_mlp, summed)
        middle_grad = upstream_low[own].astype(f32) + middle_back
        middle_grads.append(middle_grad)
        own_low = middle_grad.astype(bf16)
        middle_lows.append(jnp.concatenate([own_low, swap_core(own_low)], axis=0))
        gated_grad = product(middle_lows[micro], out_turned)
        query_grad, far_grad, kv_grad, logit_grad, query_terms = pl.pallas_call(
            functools.partial(attend_back_kernel, (micro,) + sizes),
            out_shape=(
                jax.ShapeDtypeStruct((block_rows, query_cols), bf16),
                jax.ShapeDtypeStruct((block_rows, 2 * key_cols), bf16),
                jax.ShapeDtypeStruct((block_rows, 2 * key_cols), f32),
                jax.ShapeDtypeStruct((block_rows, extra), bf16),
                jax.ShapeDtypeStruct((8, head_dim), f32),
            ),
            grid_spec=pltpu.PrefetchScalarGridSpec(
                num_scalar_prefetch=1,
                grid=(1,),
                in_specs=[
                    at_row(micro, block_rows, query_cols),
                    at_row(micro, block_rows, 2 * key_cols),
                    at_row(micro, block_rows, 2 * key_cols),
                    at_row(micro, block_rows, 2),
                    at_row(micro, 1, 2, block_rows),
                    at_row(micro, block_rows, extra),
                    at_row(micro, block_rows, query_cols),
                    at_row(micro, block_rows, extra),
                    at_row(0, block_rows, query_cols),
                    at_row(micro, block_rows, query_cols),
                    at_row(micro, block_rows, head_dim),
                    at_row(micro, block_rows, head_dim),
                    whole(2, head_dim),
                ],
                out_specs=(
                    at_row(0, block_rows, query_cols),
                    at_row(0, block_rows, 2 * key_cols),
                    at_row(0, block_rows, 2 * key_cols),
                    at_row(0, block_rows, extra),
                    at_row(0, 8, head_dim),
                ),
            ),
            compiler_params=params,
            cost_estimate=cost(
                5 * pairs, block_rows * query_cols * 30, pairs // head_dim // 2
            ),
            name="attend_back",
        )(
            prompts,
            rotated_queries,
            own_kv,
            far_kv,
            spot_cols,
            spot_rows,
            head_gate,
            attended,
            log_totals,
            gated_grad,
            projected,
            cosine,
            sine,
            head_gain,
        )
        query_gain.append(query_terms[0])
        far_grads.append(far_grad)
        joins.append((query_grad, logit_grad))
        kv_grads.append(kv_grad)
    far_grads[1] = settle(gate_up_back, far_grads[1])
    arrived = [
        lax.ppermute(
            jnp.where(offset == apart, far_grads[0], far_grads[1]),
            "dp",
            group_route(apart, (apart, (GROUP_DEVICES - 1) ^ apart)),
        )
        for apart in (1, 2, 3)
    ]
    mlp_out, kv_grads[1] = order(mlp_out, kv_grads[1])
    layer_own = (jnp.concatenate(middles) + mlp_out).astype(bf16)
    layer_own = layer_own.reshape(MICRO_BATCHES, own_rows, width)
    layer_out = place_back(layer_own, swap_core(layer_own), True, "place_layer")
    layer_out, kv_grads[0] = order(layer_out, kv_grads[0])
    *arrived, kv_grads[0], kv_grads[1] = pump(gate_up_back, *arrived, kv_grads[0], kv_grads[1])
    for micro in range(MICRO_BATCHES):
        query_grad, logit_grad = joins[micro]
        kv_grad = kv_grads[micro]
        in_grad, key_terms = pl.pallas_call(
            functools.partial(join_kernel, (micro, query_cols, key_cols, head_dim)),
            out_shape=(
                jax.ShapeDtypeStruct((block_rows, joined), bf16),
                jax.ShapeDtypeStruct((8, head_dim), f32),
            ),
            grid_spec=pltpu.PrefetchScalarGridSpec(
                num_scalar_prefetch=1,
                grid=(1,),
                in_specs=[
                    at_row(0, block_rows, query_cols),
                    at_row(0, block_rows, 2 * key_cols),
                    at_row(0, block_rows, 2 * key_cols),
                    at_row(0, block_rows, 2 * key_cols),
                    at_row(0, block_rows, 2 * key_cols),
                    at_row(0, block_rows, extra),
                    pl.BlockSpec(
                        (block_rows, key_cols),
                        lambda i, flag, micro=micro: (micro, query_cols // key_cols),
                    ),
                    at_row(micro, block_rows, head_dim),
                    at_row(micro, block_rows, head_dim),
                    whole(2, head_dim),
                ],
                out_specs=(at_row(0, block_rows, joined), at_row(0, 8, head_dim)),
            ),
            compiler_params=params,
            cost_estimate=cost(1024, 1024),
            name="join",
        )(
            prompts,
            query_grad,
            kv_grad,
            *arrived,
            logit_grad,
            projected,
            cosine,
            sine,
            head_gain,
        )
        in_grads.append(in_grad)
        key_gain_sums.append(key_terms[0])
    query_gain, key_gain_sum = query_gain[0] + query_gain[1], key_gain_sums[0] + key_gain_sums[1]
    head_gains = jnp.stack([query_gain, key_gain_sum])
    head_gains = head_gains + swap_core(head_gains)
    head_gains = head_gains + swap_x(head_gains)
    first, second, head_gains = settle(gate_up_back, *in_grads, head_gains)
    in_back = Scatter(
        lambda slot, right=jnp.concatenate((first, second)), middle_low=jnp.concatenate(
            middle_lows
        ): jnp.concatenate(
            [
                transpose_by(normed_one[:, slot * depth : (slot + 1) * depth], right),
                transpose_by(middle_low[:, slot * depth : (slot + 1) * depth], gated_all),
            ],
            axis=1,
        ),
        count,
    )
    first, second = in_back.issue(first, second)
    first = by_transpose(first, in_full).astype(bf16)
    second = by_transpose(second, in_full).astype(bf16)
    chips = [chip_sum(partial[own_rows:], partial[:own_rows]) for partial in (first, second)]
    from_x = [swap_x(chip) for chip in chips]
    chips[1], head_gains = pump(in_back, chips[1], head_gains)
    drain(gate_up_back)
    drain(down_back)
    gate_up_grad = gate_up_back.total()
    down_grad = down_back.total()
    mlp_sum = jnp.sum(
        gate_up_grad[:, :hidden_units] * gate_weight.astype(f32)
        + gate_up_grad[:, hidden_units:] * up_weight.astype(f32),
        axis=1,
    )
    gate_grad, up_grad = gate_up_grad[:, :hidden_units], gate_up_grad[:, hidden_units:]
    level, turn = 1, 0
    while level < count // 2:
        if turn == 1:
            from_x[1], gate_grad, up_grad, down_grad, mlp_sum = order(
                from_x[1], gate_grad, up_grad, down_grad, mlp_sum
            )
        late = min(turn, MICRO_BATCHES - 1)
        arrived_gains, from_x[late] = pump(in_back, swap_dp(head_gains, level), from_x[late])
        head_gains = head_gains + arrived_gains
        level, turn = 2 * level, turn + 1
    input_rows = []
    for micro in range(MICRO_BATCHES):
        part = pl.BlockSpec((own_rows // 2, width), lambda i: (i, 0))
        input_rows.append(
            pl.pallas_call(
                input_back_kernel,
                out_shape=jax.ShapeDtypeStruct((own_rows, width), f32),
                grid=(2,),
                in_specs=[
                    pl.BlockSpec(
                        (own_rows // 2, width), lambda i, micro=micro: (4 * micro + i, 0)
                    ),
                    part,
                    part,
                    whole(1, width),
                    part,
                ],
                out_specs=part,
                compiler_params=params,
                cost_estimate=cost(1024, 1024),
                name="input_back",
            )(inputs_low, chips[micro], from_x[micro], gain_attn, middle_grads[micro])
        )
    other_rows = [swap_core(rows) for rows in input_rows]
    if depth % 128:
        tokens_grad = place_back(jnp.stack(input_rows), jnp.stack(other_rows), True, "place_tokens")
    else:
        tokens_grad = pl.pallas_call(
            place_rows_kernel,
            out_shape=jax.ShapeDtypeStruct((MICRO_BATCHES, 2, own_rows, width), f32),
            grid_spec=pltpu.PrefetchScalarGridSpec(
                num_scalar_prefetch=2,
                grid=(count,),
                in_specs=[pl.BlockSpec((own_rows, depth), lambda i, cols, core: (0, i))]
                * (2 * MICRO_BATCHES),
                out_specs=pl.BlockSpec(
                    (MICRO_BATCHES, 2, own_rows, depth), lambda i, cols, core: (0, 0, 0, cols[i])
                ),
            ),
            compiler_params=params,
            cost_estimate=cost(1024, 1024),
            name="place_tokens",
        )(column_places, core_place, *input_rows, *other_rows).reshape(total_rows, width)

    arrived_gains, tokens_grad = pump(in_back, swap_dp(head_gains, level), tokens_grad)
    head_gains = head_gains + arrived_gains
    tokens_grad = drain(in_back, tokens_grad)
    in_total = in_back.total()
    in_weight_grad, out_weight_grad = in_total[:, :joined], in_total[:, joined:].T
    used = first_gain
    attn_sum = jnp.sum(in_weight_grad[:, :used] * packed[:, :used].astype(f32), axis=1)
    gains = jnp.stack([attn_sum, mlp_sum])
    for swap in (swap_core, swap_x):
        gains = gains + swap(gains)
    return (
        layer_out,
        tokens_grad,
        in_weight_grad[:, :query_cols],
        in_weight_grad[:, query_cols : query_cols + key_cols],
        in_weight_grad[:, query_cols + key_cols : query_cols + 2 * key_cols],
        in_weight_grad[:, query_cols + 2 * key_cols : query_cols + 2 * key_cols + head_count],
        out_weight_grad,
        gate_grad,
        up_grad,
        down_grad,
        gains[0] / norm_attn.astype(f32),
        gains[1] / norm_mlp.astype(f32),
        head_gains[0],
        head_gains[1],
    )


def solution(mesh):
    rows, weight, turned = P("dp", None), P("dp", "mp"), P("mp", "dp")
    weights = (weight, weight, weight, weight, turned, weight, weight, turned)
    placed = (rows, rows) + weights + (P("dp"), P("dp"), P(), P())
    return jax.shard_map(
        on_device, mesh=mesh, in_specs=placed + (P(),), out_specs=placed, check_vma=False
    )
```

```python
import functools

import jax
import jax.numpy as jnp
from jax import lax
from jax.experimental import pallas as pl
from jax.experimental.pallas import tpu as pltpu
from jax.sharding import PartitionSpec as P

MICRO_BATCHES = 2
GROUP_DEVICES = 4

eps = 1e-06
rope_base = 1000000.0
masked = -1e30
f32 = jnp.float32
bf16 = jnp.bfloat16


def product(left_side, right_side):
    return jnp.dot(left_side, right_side, preferred_element_type=f32)


def by_transpose(left_side, right_side):
    return lax.dot_general(
        left_side, right_side, (((1,), (1,)), ((), ())), preferred_element_type=f32
    )


def transpose_by(left_side, right_side):
    return lax.dot_general(
        left_side, right_side, (((0,), (0,)), ((), ())), preferred_element_type=f32
    )


def recip_rms(values):
    return lax.rsqrt(jnp.mean(values * values, axis=-1, keepdims=True) + eps)


def rms_back(values, reciprocal, gain, gradient):
    scaled = gain * gradient
    cubed = reciprocal * reciprocal * reciprocal
    back = reciprocal * scaled - values * cubed * jnp.mean(scaled * values, axis=-1, keepdims=True)
    return (back, gradient * values * reciprocal)


def layout(lengths, relative, row_count):
    seg_ends = jnp.cumsum(lengths, dtype=jnp.int32)
    starts = seg_ends - lengths
    row_ids = jnp.arange(row_count, dtype=jnp.int32)
    seg_index = jnp.sum(
        (row_ids[:, None] >= seg_ends[None, :]).astype(jnp.int32), axis=1, dtype=jnp.int32
    )
    seg_onehot = seg_index[:, None] == jnp.arange(lengths.shape[0], dtype=jnp.int32)[None, :]
    seg_start = jnp.sum(jnp.where(seg_onehot, starts[None, :], 0), axis=1, dtype=jnp.int32)
    prompt = relative == 0
    segment = jnp.where(prompt, 0, 1 + seg_index)
    position = jnp.where(prompt, row_ids, row_count + row_ids - seg_start)
    return (segment, position)


def ring_order(count):
    return list(range(0, count, 2)) + list(range(count - 1, 0, -2))


def ring_step(block, count, forward):
    places = ring_order(count)
    turn = 1 if forward else -1
    route = [(places[i], places[(i + turn) % count]) for i in range(count)]
    return lax.ppermute(block, "dp", route)


class Gather:
    def __init__(self, block, count):
        self.count = count
        self.left = count // 2
        self.cut = (block.shape[1] // 256) * 128
        self.held = [[block], [block]]
        self.flying = []

    def issue(self):
        if self.left:
            self.left -= 1
            ahead, behind = self.held[0][-1], self.held[1][-1]
            if not self.left:
                ahead, behind = ahead[:, : self.cut], behind[:, self.cut :]
            self.flying = [
                (0, ring_step(ahead, self.count, True)),
                (1, ring_step(behind, self.count, False)),
            ]

    def land(self, arrays):
        for (way, _), array in zip(self.flying, arrays):
            self.held[way].append(array)
        self.flying = []

    def gathered(self, first, end):
        ahead, behind = self.held
        half = self.count // 2
        near = [ahead[step] for step in range(half - 1, -1, -1)]
        near += [behind[step] for step in range(1, half)]
        near.append(jnp.concatenate([ahead[half], behind[half]], axis=1))
        return jnp.concatenate([block[:, first:end] for block in near], axis=0)


class Scatter:
    def __init__(self, chunk, count, split=True):
        half = count // 2
        self.count, self.chunk, self.split = count, chunk, split
        self.own = half - 1
        self.left = half
        self.got = [None, None]
        self.flying = []

    def issue(self, *values):
        parts = []
        if self.left == self.count // 2:
            far = self.chunk(self.own + self.left).astype(bf16)
            cut = far.shape[1] // 256 * 128 or far.shape[1] // 2
            if self.split:
                parts = [(0, far[:, :cut]), (1, far[:, cut:])]
            else:
                ahead = self.chunk(self.own + self.left - 1).astype(bf16)
                parts = [(0, ahead), (1, far)]
        elif self.left > 0:
            late = 0 if self.split else 1
            for way, slot in ((0, self.own + self.left - late), (1, self.own - self.left)):
                if slot == self.own:
                    self.kept = self.got[way]
                    continue
                part, got = self.chunk(slot), self.got[way].astype(f32)
                lack = part.shape[1] - got.shape[1]
                if lack:
                    got = jnp.pad(got, ((0, 0), ((0, lack), (lack, 0))[way]))
                parts.append((way, (part + got).astype(bf16)))
        self.left -= 1
        if parts and values:
            tied = lax.optimization_barrier(tuple(part for _, part in parts) + values)
            parts = [(way, part) for (way, _), part in zip(parts, tied)]
            values = tied[len(parts) :]
        self.flying = [(way, ring_step(part, self.count, way == 0)) for way, part in parts]
        return values

    def land(self, arrays):
        for (way, _), array in zip(self.flying, arrays):
            self.got[way] = array
        self.flying = []

    def total(self):
        if not self.split:
            self.got[0] = self.kept
        return self.chunk(self.own) + self.got[0].astype(f32) + self.got[1].astype(f32)


def single(values):
    return values[0] if len(values) == 1 else values


def pump(ring, *values):
    arrays = [array for _, array in ring.flying]
    if arrays and values:
        tied = lax.optimization_barrier(tuple(arrays) + values)
        arrays, values = list(tied[: len(arrays)]), tied[len(arrays) :]
    ring.land(arrays)
    if isinstance(ring, Scatter):
        values = ring.issue(*values)
    else:
        ring.issue()
    return single(values)


def settle(ring, *values):
    arrays = [array for _, array in ring.flying]
    tied = lax.optimization_barrier(tuple(arrays) + values)
    ring.land(list(tied[: len(arrays)]))
    return single(tied[len(arrays) :])


def drain(ring, *values):
    while ring.flying or ring.left > 0:
        values = pump(ring, *values)
        values = values if isinstance(values, tuple) else (values,)
    return single(values)


def order(*values):
    return lax.optimization_barrier(values)


def swap_core(block):
    return lax.ppermute(block, "mp", [(i, i ^ 1) for i in range(lax.axis_size("mp"))])


def swap_x(block):
    return lax.ppermute(block, "mp", [(i, i ^ 2) for i in range(lax.axis_size("mp"))])


def swap_dp(block, level):
    count = lax.axis_size("dp")
    return lax.ppermute(block, "dp", [(i, i ^ level) for i in range(count)])


def chip_sum(other_part, own_part):
    return (own_part + swap_core(other_part.astype(bf16)).astype(f32)).astype(bf16)


def across(other_part, own_part):
    chip = chip_sum(other_part, own_part)
    return chip.astype(f32) + swap_x(chip).astype(f32)


def group_route(apart, sources):
    count = lax.axis_size("dp")
    route = []
    for base in range(0, count, GROUP_DEVICES):
        route += [(base + s, base + (s ^ apart)) for s in sources]
    return route

def by_row(*shape):
    return pl.BlockSpec(shape, lambda i, *rest: (i,) + (0,) * (len(shape) - 1))


def at_row(place, *shape):
    return pl.BlockSpec(shape, lambda i, *rest: (place,) + (0,) * (len(shape) - 1))


def whole(*shape):
    return pl.BlockSpec(shape, lambda *at: (0,) * len(shape))


def turned(values, cosine, sine):
    return values * cosine + pltpu.roll(values, values.shape[-1] // 2, 1) * sine


def bring_kernel(columns_ref, core_ref, in_ref, out_ref):
    core = core_ref[0]
    out_ref[:, 0:1] = in_ref[:, pl.ds(core, 1)]
    out_ref[:, 1:2] = in_ref[:, pl.ds(1 - core, 1)]


def place_kernel(columns_ref, core_ref, own_ref, other_ref, out_ref):
    core = core_ref[0]
    out_ref[:, pl.ds(core, 1)] = own_ref[...][:, None]
    out_ref[:, pl.ds(1 - core, 1)] = other_ref[...][:, None]


def place_rows_kernel(columns_ref, core_ref, *refs):
    core, out_ref = core_ref[0], refs[-1]
    for micro in range(MICRO_BATCHES):
        out_ref[micro, pl.ds(core, 1)] = refs[micro][...][None]
        out_ref[micro, pl.ds(1 - core, 1)] = refs[MICRO_BATCHES + micro][...][None]


def input_back_kernel(input_ref, chip_ref, other_ref, gain_ref, base_ref, out_ref):
    values = input_ref[...].astype(f32)
    gradient = chip_ref[...].astype(f32) + other_ref[...].astype(f32)
    back, _ = rms_back(values, recip_rms(values), gain_ref[...], gradient)
    out_ref[...] = base_ref[...] + back


def pack_kernel(*refs):
    out_ref, start = refs[-1], 0
    for ref in refs[:-2]:
        end = start + ref.shape[1]
        out_ref[:, start:end] = ref[...]
        start = end
    out_ref[:, start:] = refs[-2][...].T


def heads_kernel(sizes, proj_ref, cos_ref, sin_ref, gain_ref, q_ref, kv_ref, gate_ref):
    query_cols, key_cols, head_dim = sizes
    cosine, sine = cos_ref[...], sin_ref[...]
    for start in range(0, query_cols + key_cols, head_dim):
        values = proj_ref[:, start : start + head_dim]
        gain = gain_ref[0:1] if start < query_cols else gain_ref[1:2]
        low = turned(values * recip_rms(values) * gain, cosine, sine).astype(bf16)
        if start < query_cols:
            q_ref[:, start : start + head_dim] = low
        else:
            kv_ref[:, start - query_cols : start - query_cols + head_dim] = low
    values = proj_ref[:, query_cols + key_cols : query_cols + 2 * key_cols]
    kv_ref[:, key_cols:] = values.astype(bf16)
    gate_ref[...] = jax.nn.sigmoid(proj_ref[:, query_cols + 2 * key_cols :])


def attend_kernel(
    sizes, flag_ref, q_ref, kv_ref, far_ref, col_ref, row_ref, gate_ref, gated_ref, att_ref, lse_ref
):
    head_dim, key_cols, kv_heads, repeat_heads, scale = sizes
    no_far = jnp.where(flag_ref[pl.program_id(0)] == 1, masked, 0.0)
    columns, rows = col_ref[...], row_ref[0]
    own = (columns[:, 0:1] == rows[0:1]) & (rows[1:2] <= columns[:, 1:2])
    for kv_head in range(kv_heads):
        at = slice(kv_head * head_dim, (kv_head + 1) * head_dim)
        at_value = slice(key_cols + kv_head * head_dim, key_cols + (kv_head + 1) * head_dim)
        for head in range(kv_head * repeat_heads, (kv_head + 1) * repeat_heads):
            here = slice(head * head_dim, (head + 1) * head_dim)
            queries = q_ref[:, here]
            far = by_transpose(queries, far_ref[:, at]) * scale + no_far
            near = jnp.where(own, by_transpose(queries, kv_ref[:, at]) * scale, masked)
            peak = jnp.maximum(
                jnp.max(far, axis=-1, keepdims=True), jnp.max(near, axis=-1, keepdims=True)
            )
            far = jnp.exp(far - peak)
            near = jnp.exp(near - peak)
            total = jnp.sum(far, axis=-1, keepdims=True) + jnp.sum(near, axis=-1, keepdims=True)
            share = 1.0 / total
            attended = product((far * share).astype(bf16), far_ref[:, at_value]) + product(
                (near * share).astype(bf16), kv_ref[:, at_value]
            )
            att_ref[:, here] = attended
            gated_ref[:, here] = (attended * gate_ref[:, head : head + 1]).astype(bf16)
            lse_ref[:, head : head + 1] = peak + jnp.log(total)


def attend_back_kernel(
    sizes,
    flag_ref,
    q_ref,
    kv_ref,
    far_ref,
    col_ref,
    row_ref,
    gate_ref,
    att_ref,
    lse_ref,
    grad_ref,
    proj_ref,
    cos_ref,
    sin_ref,
    gain_ref,
    dq_ref,
    dfar_ref,
    dkv_ref,
    logit_ref,
    dgain_ref,
):
    micro, head_dim, key_cols, kv_heads, repeat_heads, scale = sizes
    no_far = jnp.where(flag_ref[micro] == 1, masked, 0.0)
    columns, rows = col_ref[...], row_ref[0]
    own = (columns[:, 0:1] == rows[0:1]) & (columns[:, 1:2] <= rows[1:2])
    cosine, sine, gain = cos_ref[...], sin_ref[...], gain_ref[0:1]
    logit_ref[...] = jnp.zeros_like(logit_ref)
    lane = lax.broadcasted_iota(jnp.int32, lse_ref.shape, 1)
    deltas = jnp.zeros(lse_ref.shape, f32)
    lows = []
    for head in range(kv_heads * repeat_heads):
        here = slice(head * head_dim, (head + 1) * head_dim)
        gate = gate_ref[:, head : head + 1]
        gated_grad, attended = grad_ref[:, here], att_ref[:, here]
        weighted = jnp.sum(gated_grad * attended, axis=-1, keepdims=True)
        logit_ref[:, head : head + 1] = (weighted * gate * (1.0 - gate)).astype(bf16)
        low = (gated_grad * gate).astype(bf16)
        delta = jnp.sum(low.astype(f32) * attended, axis=-1, keepdims=True)
        deltas = jnp.where(lane == head, delta, deltas)
        lows.append(low)
    deltas, totals_log = deltas.T, lse_ref[...].T
    gain_sum = jnp.zeros((1, head_dim), f32)
    for kv_head in range(kv_heads):
        at = slice(kv_head * head_dim, (kv_head + 1) * head_dim)
        at_value = slice(key_cols + kv_head * head_dim, key_cols + (kv_head + 1) * head_dim)
        totals = [0.0, 0.0, 0.0, 0.0]
        for head in range(kv_head * repeat_heads, (kv_head + 1) * repeat_heads):
            here = slice(head * head_dim, (head + 1) * head_dim)
            queries, low = q_ref[:, here], lows[head]
            delta, log_total = deltas[head : head + 1], totals_log[head : head + 1]
            far = jnp.exp(by_transpose(far_ref[:, at], queries) * scale + (no_far - log_total))
            near = by_transpose(kv_ref[:, at], queries) * scale
            near = jnp.exp(jnp.where(own, near - log_total, masked))
            far_low = (far * (by_transpose(far_ref[:, at_value], low) - delta)).astype(bf16)
            near_low = (near * (by_transpose(kv_ref[:, at_value], low) - delta)).astype(bf16)
            totals[0] = totals[0] + product(far_low, queries)
            totals[1] = totals[1] + product(far.astype(bf16), low)
            totals[2] = totals[2] + product(near_low, queries)
            totals[3] = totals[3] + product(near.astype(bf16), low)
            back = transpose_by(far_low, far_ref[:, at]) + transpose_by(near_low, kv_ref[:, at])
            back = back * scale
            values = proj_ref[:, here]
            back, terms = rms_back(
                values, recip_rms(values), gain, turned(back, cosine, -sine)
            )
            dq_ref[:, here] = back.astype(bf16)
            gain_sum = gain_sum + jnp.sum(terms, axis=0, keepdims=True)
        dfar_ref[:, at] = (totals[0] * scale).astype(bf16)
        dfar_ref[:, at_value] = totals[1].astype(bf16)
        dkv_ref[:, at] = totals[2] * scale
        dkv_ref[:, at_value] = totals[3]
    dgain_ref[...] = jnp.broadcast_to(gain_sum, dgain_ref.shape)


def join_kernel(
    sizes,
    flag_ref,
    dq_ref,
    dkv_ref,
    one_ref,
    two_ref,
    three_ref,
    logit_ref,
    proj_ref,
    cos_ref,
    sin_ref,
    gain_ref,
    out_ref,
    dgain_ref,
):
    micro, query_cols, key_cols, head_dim = sizes
    prompt = flag_ref[micro] == 1
    cosine, sine, gain = cos_ref[...], sin_ref[...], gain_ref[1:2]
    out_ref[:, :query_cols] = dq_ref[...]
    out_ref[:, query_cols + 2 * key_cols :] = logit_ref[...]
    gain_sum = jnp.zeros((1, head_dim), f32)
    for start in range(0, 2 * key_cols, head_dim):
        at = slice(start, start + head_dim)
        arrived = one_ref[:, at].astype(f32) + two_ref[:, at].astype(f32)
        arrived = arrived + three_ref[:, at].astype(f32)
        total = dkv_ref[:, at] + jnp.where(prompt, arrived, 0.0)
        if start < key_cols:
            values = proj_ref[:, at]
            total, terms = rms_back(
                values, recip_rms(values), gain, turned(total, cosine, -sine)
            )
            gain_sum = gain_sum + jnp.sum(terms, axis=0, keepdims=True)
        out_ref[:, query_cols + start : query_cols + start + head_dim] = total.astype(bf16)
    dgain_ref[...] = jnp.broadcast_to(gain_sum, dgain_ref.shape)


def cost(flops, nbytes, exps=0):
    return pl.CostEstimate(flops=flops, bytes_accessed=nbytes, transcendentals=exps)


vmem_bytes = 56 << 20


def on_device(
    tokens,
    cotangent,
    query_weight,
    key_matrix,
    value_matrix,
    head_gate_weight,
    out_weight,
    gate_weight,
    up_weight,
    down_weight,
    norm_attn,
    norm_mlp,
    norm_query,
    norm_key,
    cont_lengths,
):
    count = lax.axis_size("dp")
    dp_index = lax.axis_index("dp")
    core = lax.axis_index("mp") % 2
    place = jnp.where(dp_index % 2 == 0, dp_index // 2, count - 1 - dp_index // 2)
    offset = dp_index % GROUP_DEVICES
    group_index = dp_index // GROUP_DEVICES
    total_rows, width = tokens.shape
    block_rows = total_rows // MICRO_BATCHES
    own_rows = block_rows // 2
    depth = width // count
    head_dim = norm_query.shape[0]
    head_count = head_gate_weight.shape[1]
    query_cols = query_weight.shape[1]
    key_cols = key_matrix.shape[1]
    kv_heads = key_cols // head_dim
    repeat_heads = head_count // kv_heads
    hidden_units = gate_weight.shape[1]
    score_scale = head_dim ** (-0.5)
    gain_query = norm_query.astype(f32)
    key_gain = norm_key.astype(f32)
    first_place = (place + count - (count // 2 - 1)) % count
    places = ring_order(count)

    extra = 128
    lane = lax.broadcasted_iota(jnp.int32, (depth, extra), 1)
    small = jnp.pad(head_gate_weight, ((0, 0), (0, extra - head_count)))
    small = jnp.where(lane == head_count, norm_attn[:, None], small)
    small = jnp.where(lane == head_count + 1, norm_mlp[:, None], small)
    parts = (query_weight, key_matrix, value_matrix, small)
    packed_cols = sum(part.shape[1] for part in parts)
    in_block = pl.pallas_call(
        pack_kernel,
        out_shape=jax.ShapeDtypeStruct((depth, packed_cols + out_weight.shape[0]), bf16),
        compiler_params=pltpu.CompilerParams(vmem_limit_bytes=vmem_bytes),
        cost_estimate=cost(1024, 1024),
        name="pack",
    )(*parts, out_weight)
    packed = in_block[:, :packed_cols]
    in_ring = Gather(in_block, count)
    in_ring.issue()

    params = pltpu.CompilerParams(vmem_limit_bytes=vmem_bytes)
    column_places = jnp.asarray(places, jnp.int32)[
        (first_place + jnp.arange(count, dtype=jnp.int32)) % count
    ]
    core_place = core.astype(jnp.int32)[None]

    def rows_in(block):
        halves = block.reshape((MICRO_BATCHES, 2, own_rows) + block.shape[1:])
        swapped = jnp.concatenate([halves[:, 1:], halves[:, :1]], axis=1)
        return jnp.where(core == 0, halves, swapped).reshape(block.shape)

    def bring(block, name):
        if depth % 128:
            ring = [block[:, i * depth : (i + 1) * depth] for i in places]
            block = lax.dynamic_slice_in_dim(
                jnp.concatenate(ring + ring, axis=1), first_place * depth, width, axis=1
            )
            return rows_in(block)
        shape = (MICRO_BATCHES, 2, own_rows, width)
        there = (MICRO_BATCHES, 2, own_rows, depth)
        return pl.pallas_call(
            bring_kernel,
            out_shape=jax.ShapeDtypeStruct(shape, block.dtype),
            grid_spec=pltpu.PrefetchScalarGridSpec(
                num_scalar_prefetch=2,
                grid=(count,),
                in_specs=[pl.BlockSpec(there, lambda i, cols, core: (0, 0, 0, cols[i]))],
                out_specs=pl.BlockSpec(there, lambda i, cols, core: (0, 0, 0, i)),
            ),
            compiler_params=params,
            cost_estimate=cost(0, 2 * block.size * block.dtype.itemsize),
            name=name,
        )(column_places, core_place, block.reshape(shape)).reshape(block.shape)

    def columns_back(block):
        back = lax.dynamic_slice_in_dim(
            jnp.concatenate([block, block], axis=-1),
            ((count - first_place) % count) * depth,
            width,
            axis=-1,
        )
        at = {device: i for i, device in enumerate(places)}
        return jnp.concatenate(
            [back[..., at[i] * depth : (at[i] + 1) * depth] for i in range(count)], axis=-1
        )

    def place_back(own, other, turned, name):
        if depth % 128:
            low = jnp.where(core == 0, own, other)
            high = jnp.where(core == 0, other, own)
            block = jnp.stack([low, high], axis=1).reshape(total_rows, width)
            return columns_back(block) if turned else block
        there = (MICRO_BATCHES, own_rows, depth)
        return pl.pallas_call(
            place_kernel,
            out_shape=jax.ShapeDtypeStruct((MICRO_BATCHES, 2, own_rows, width), own.dtype),
            grid_spec=pltpu.PrefetchScalarGridSpec(
                num_scalar_prefetch=2,
                grid=(count,),
                in_specs=[pl.BlockSpec(there, lambda i, cols, core: (0, 0, i))] * 2,
                out_specs=pl.BlockSpec(
                    (MICRO_BATCHES, 2, own_rows, depth),
                    lambda i, cols, core: (0, 0, 0, cols[i] if turned else i),
                ),
            ),
            compiler_params=params,
            cost_estimate=cost(1024, 1024),
            name=name,
        )(column_places, core_place, own, other).reshape(total_rows, width)

    inputs_low = bring(tokens, "bring_tokens")

    inverse = jnp.power(rope_base, -jnp.arange(head_dim // 2, dtype=f32) * (2.0 / head_dim))
    relatives, segments, positions = [], [], []
    for micro in range(MICRO_BATCHES):
        holder = GROUP_DEVICES - 1 if micro % 2 == 1 else 0
        relative = jnp.bitwise_xor(offset, holder)
        lengths = cont_lengths[group_index, jnp.maximum(relative - 1, 0), micro]
        segment, position = layout(lengths, relative, block_rows)
        relatives.append(relative)
        segments.append(segment)
        positions.append(position)
    segment = rows_in(jnp.concatenate(segments))
    position = rows_in(jnp.concatenate(positions))
    angles = position.astype(f32)[:, None] * inverse[None, :]
    inputs_low, angles = pump(in_ring, inputs_low, angles)
    inputs = inputs_low.astype(f32)
    recip_one = recip_rms(inputs)
    recip_one, cotangent, late_down = pump(in_ring, recip_one, cotangent, down_weight)
    mlp_block = jnp.concatenate([gate_weight, up_weight, late_down.T], axis=1)
    cosine, sine = jnp.cos(angles), jnp.sin(angles)
    cosine = jnp.concatenate([cosine, cosine], axis=1)
    sine = jnp.concatenate([-sine, sine], axis=1)
    spots = jnp.stack([segment, position])
    spot_cols = spots.T
    spot_rows = spots.reshape(2, MICRO_BATCHES, block_rows).transpose(1, 0, 2)
    prompts = jnp.stack([(r == 0).astype(jnp.int32) for r in relatives])
    head_gain = jnp.stack([gain_query, key_gain])

    recip_one, cosine, sine, mlp_block = pump(in_ring, recip_one, cosine, sine, mlp_block)
    recip_one, mlp_block = drain(in_ring, recip_one, mlp_block)
    mlp_ring = Gather(mlp_block, count)
    mlp_ring.issue()
    joined = packed.shape[1]
    in_full = in_ring.gathered(0, joined)
    out_turned = in_ring.gathered(joined, joined + query_cols)
    first_gain = query_cols + 2 * key_cols + head_count
    gain_attn = in_full[:, first_gain].astype(f32)[None, :]
    gain_mlp = in_full[:, first_gain + 1].astype(f32)[None, :]
    normed_one = (inputs * recip_one * gain_attn).astype(bf16)
    projected = product(normed_one, in_full)
    rotated_queries, own_kv, head_gate = pl.pallas_call(
        functools.partial(heads_kernel, (query_cols, key_cols, head_dim)),
        out_shape=(
            jax.ShapeDtypeStruct((total_rows, query_cols), bf16),
            jax.ShapeDtypeStruct((total_rows, 2 * key_cols), bf16),
            jax.ShapeDtypeStruct((total_rows, extra), f32),
        ),
        grid=(total_rows // own_rows,),
        in_specs=[
            by_row(own_rows, joined),
            by_row(own_rows, head_dim),
            by_row(own_rows, head_dim),
            whole(2, head_dim),
        ],
        out_specs=(
            by_row(own_rows, query_cols),
            by_row(own_rows, 2 * key_cols),
            by_row(own_rows, extra),
        ),
        compiler_params=params,
        cost_estimate=cost(total_rows * joined * 20, total_rows * joined * 7),
        name="heads",
    )(projected, cosine, sine, head_gain)

    first_kv, second_kv = own_kv[:block_rows], own_kv[block_rows:]
    sent = jnp.where(offset == 0, first_kv, second_kv)
    by_one = lax.ppermute(sent, "dp", group_route(1, (0, 3)))
    by_two = lax.ppermute(sent, "dp", group_route(2, (0, 3)))
    by_both = lax.ppermute(sent, "dp", group_route(3, (0, 3)))
    far_kv = [
        jnp.where(offset == 1, by_one, jnp.where(offset == 2, by_two, by_both)),
        jnp.where(offset == 2, by_one, jnp.where(offset == 1, by_two, by_both)),
    ]

    far_kv = jnp.concatenate(far_kv, axis=0)
    far_kv, cotangent = pump(mlp_ring, far_kv, cotangent)
    sizes = (head_dim, key_cols, kv_heads, repeat_heads, score_scale)
    pairs = total_rows * 2 * block_rows * query_cols
    gated_all, attended, log_totals = pl.pallas_call(
        functools.partial(attend_kernel, sizes),
        out_shape=(
            jax.ShapeDtypeStruct((total_rows, query_cols), bf16),
            jax.ShapeDtypeStruct((total_rows, query_cols), f32),
            jax.ShapeDtypeStruct((total_rows, extra), f32),
        ),
        grid_spec=pltpu.PrefetchScalarGridSpec(
            num_scalar_prefetch=1,
            grid=(MICRO_BATCHES, 2),
            in_specs=[
                pl.BlockSpec((own_rows, query_cols), lambda m, i, flag: (2 * m + i, 0)),
                pl.BlockSpec((block_rows, 2 * key_cols), lambda m, i, flag: (m, 0)),
                pl.BlockSpec((block_rows, 2 * key_cols), lambda m, i, flag: (m, 0)),
                pl.BlockSpec((own_rows, 2), lambda m, i, flag: (2 * m + i, 0)),
                pl.BlockSpec((1, 2, block_rows), lambda m, i, flag: (m, 0, 0)),
                pl.BlockSpec((own_rows, extra), lambda m, i, flag: (2 * m + i, 0)),
            ],
            out_specs=(
                pl.BlockSpec((own_rows, query_cols), lambda m, i, flag: (2 * m + i, 0)),
                pl.BlockSpec((own_rows, query_cols), lambda m, i, flag: (2 * m + i, 0)),
                pl.BlockSpec((own_rows, extra), lambda m, i, flag: (2 * m + i, 0)),
            ),
        ),
        compiler_params=params,
        cost_estimate=cost(4 * pairs, total_rows * query_cols * 12, pairs // head_dim),
        name="attend",
    )(prompts, rotated_queries, own_kv, far_kv, spot_cols, spot_rows, head_gate)

    gated_all, cotangent = order(gated_all, cotangent)
    upstream_low = bring(cotangent, "bring_cotangent")
    gated_all, upstream_low = pump(mlp_ring, gated_all, upstream_low)
    middles, recips_two, norms_two = [], [], []
    for micro in range(MICRO_BATCHES):
        base = micro * block_rows
        gated_low = gated_all[base : base + block_rows]
        summed = across(
            by_transpose(gated_low[own_rows:], out_turned),
            by_transpose(gated_low[:own_rows], out_turned),
        )
        middle = inputs[base : base + own_rows] + summed
        recip_two = recip_rms(middle)
        own_norm = (middle * recip_two * gain_mlp).astype(bf16)
        if micro == 0:
            own_norm = pump(mlp_ring, own_norm)
        middles.append(middle)
        recips_two.append(recip_two)
        norms_two += [own_norm, swap_core(own_norm)]
    normed_two = jnp.concatenate(norms_two, axis=0)
    normed_two = drain(mlp_ring, normed_two)
    gate_up_full = mlp_ring.gathered(0, 2 * hidden_units)
    down_turned = mlp_ring.gathered(2 * hidden_units, 3 * hidden_units)
    pre = product(normed_two, gate_up_full).astype(bf16)
    gate_pre, up_pre = pre[:, :hidden_units].astype(f32), pre[:, hidden_units:].astype(f32)
    sigmoid_gate = jax.nn.sigmoid(gate_pre)
    swish_gate = gate_pre * sigmoid_gate
    hidden_low = (swish_gate * up_pre).astype(bf16)
    down_back = Scatter(
        lambda slot, left=hidden_low, right=upstream_low: transpose_by(
            left, right[:, slot * depth : (slot + 1) * depth]
        ),
        count,
        False,
    )
    (upstream_late,) = down_back.issue(upstream_low)
    hidden_grad = product(upstream_late, down_turned)
    gate_grad = (
        hidden_grad * up_pre * sigmoid_gate * (1.0 + gate_pre * (1.0 - sigmoid_gate))
    ).astype(bf16)
    up_grad = (hidden_grad * swish_gate).astype(bf16)
    gate_grad, up_grad = pump(down_back, gate_grad, up_grad)
    gate_up_grad = jnp.concatenate([gate_grad, up_grad], axis=1)
    partial = by_transpose(gate_up_grad, gate_up_full).astype(bf16)
    partial, gate_up_late = pump(down_back, partial, gate_up_grad)
    gate_up_back = Scatter(
        lambda slot, left=normed_two, right=gate_up_late: transpose_by(
            left[:, slot * depth : (slot + 1) * depth], right
        ),
        count,
    )
    parts = [partial[i * own_rows : (i + 1) * own_rows] for i in range(2 * MICRO_BATCHES)]
    from_other = swap_core(jnp.concatenate(parts[1::2]))
    chips = [
        (parts[2 * i].astype(f32) + from_other[i * own_rows : (i + 1) * own_rows].astype(f32)).astype(
            bf16
        )
        for i in range(MICRO_BATCHES)
    ]
    summed_parts = [part.astype(f32) + swap_x(part).astype(f32) for part in chips]
    (hidden_late,) = gate_up_back.issue(hidden_low)
    hidden_late = pump(down_back, hidden_late)
    parts = [hidden_late[i * own_rows : (i + 1) * own_rows] for i in range(2 * MICRO_BATCHES)]
    mlp_other = by_transpose(jnp.concatenate(parts[1::2]), down_turned).astype(bf16)
    mlp_own = by_transpose(jnp.concatenate(parts[::2]), down_turned).astype(bf16)
    mlp_out = across(mlp_other, mlp_own)

    middle_grads, middle_lows = [], []
    in_grads, query_gain, key_gain_sums, joins, far_grads, kv_grads = [], [], [], [], [], []
    for micro in range(MICRO_BATCHES):
        base = micro * block_rows
        own, other = slice(base, base + own_rows), slice(base + own_rows, base + block_rows)
        summed = summed_parts[micro]
        if micro == 0:
            summed = drain(down_back, summed)
            summed = pump(gate_up_back, summed)
        else:
            kv_grads[0], summed = pump(gate_up_back, kv_grads[0], summed)
        middle_back, _ = rms_back(middles[micro], recips_two[micro], gain_mlp, summed)
        middle_grad = upstream_low[own].astype(f32) + middle_back
        middle_grads.append(middle_grad)
        own_low = middle_grad.astype(bf16)
        middle_lows.append(jnp.concatenate([own_low, swap_core(own_low)], axis=0))
        gated_grad = product(middle_lows[micro], out_turned)
        query_grad, far_grad, kv_grad, logit_grad, query_terms = pl.pallas_call(
            functools.partial(attend_back_kernel, (micro,) + sizes),
            out_shape=(
                jax.ShapeDtypeStruct((block_rows, query_cols), bf16),
                jax.ShapeDtypeStruct((block_rows, 2 * key_cols), bf16),
                jax.ShapeDtypeStruct((block_rows, 2 * key_cols), f32),
                jax.ShapeDtypeStruct((block_rows, extra), bf16),
                jax.ShapeDtypeStruct((8, head_dim), f32),
            ),
            grid_spec=pltpu.PrefetchScalarGridSpec(
                num_scalar_prefetch=1,
                grid=(1,),
                in_specs=[
                    at_row(micro, block_rows, query_cols),
                    at_row(micro, block_rows, 2 * key_cols),
                    at_row(micro, block_rows, 2 * key_cols),
                    at_row(micro, block_rows, 2),
                    at_row(micro, 1, 2, block_rows),
                    at_row(micro, block_rows, extra),
                    at_row(micro, block_rows, query_cols),
                    at_row(micro, block_rows, extra),
                    at_row(0, block_rows, query_cols),
                    at_row(micro, block_rows, query_cols),
                    at_row(micro, block_rows, head_dim),
                    at_row(micro, block_rows, head_dim),
                    whole(2, head_dim),
                ],
                out_specs=(
                    at_row(0, block_rows, query_cols),
                    at_row(0, block_rows, 2 * key_cols),
                    at_row(0, block_rows, 2 * key_cols),
                    at_row(0, block_rows, extra),
                    at_row(0, 8, head_dim),
                ),
            ),
            compiler_params=params,
            cost_estimate=cost(
                5 * pairs, block_rows * query_cols * 30, pairs // head_dim // 2
            ),
            name="attend_back",
        )(
            prompts,
            rotated_queries,
            own_kv,
            far_kv,
            spot_cols,
            spot_rows,
            head_gate,
            attended,
            log_totals,
            gated_grad,
            projected,
            cosine,
            sine,
            head_gain,
        )
        query_gain.append(query_terms[0])
        far_grads.append(far_grad)
        joins.append((query_grad, logit_grad))
        kv_grads.append(kv_grad)
    far_grads[1] = settle(gate_up_back, far_grads[1])
    arrived = [
        lax.ppermute(
            jnp.where(offset == apart, far_grads[0], far_grads[1]),
            "dp",
            group_route(apart, (apart, (GROUP_DEVICES - 1) ^ apart)),
        )
        for apart in (1, 2, 3)
    ]
    mlp_out, kv_grads[1] = order(mlp_out, kv_grads[1])
    layer_own = (jnp.concatenate(middles) + mlp_out).astype(bf16)
    layer_own = layer_own.reshape(MICRO_BATCHES, own_rows, width)
    layer_out = place_back(layer_own, swap_core(layer_own), True, "place_layer")
    layer_out, kv_grads[0] = order(layer_out, kv_grads[0])
    *arrived, kv_grads[0], kv_grads[1] = pump(gate_up_back, *arrived, kv_grads[0], kv_grads[1])
    for micro in range(MICRO_BATCHES):
        query_grad, logit_grad = joins[micro]
        kv_grad = kv_grads[micro]
        in_grad, key_terms = pl.pallas_call(
            functools.partial(join_kernel, (micro, query_cols, key_cols, head_dim)),
            out_shape=(
                jax.ShapeDtypeStruct((block_rows, joined), bf16),
                jax.ShapeDtypeStruct((8, head_dim), f32),
            ),
            grid_spec=pltpu.PrefetchScalarGridSpec(
                num_scalar_prefetch=1,
                grid=(1,),
                in_specs=[
                    at_row(0, block_rows, query_cols),
                    at_row(0, block_rows, 2 * key_cols),
                    at_row(0, block_rows, 2 * key_cols),
                    at_row(0, block_rows, 2 * key_cols),
                    at_row(0, block_rows, 2 * key_cols),
                    at_row(0, block_rows, extra),
                    pl.BlockSpec(
                        (block_rows, key_cols),
                        lambda i, flag, micro=micro: (micro, query_cols // key_cols),
                    ),
                    at_row(micro, block_rows, head_dim),
                    at_row(micro, block_rows, head_dim),
                    whole(2, head_dim),
                ],
                out_specs=(at_row(0, block_rows, joined), at_row(0, 8, head_dim)),
            ),
            compiler_params=params,
            cost_estimate=cost(1024, 1024),
            name="join",
        )(
            prompts,
            query_grad,
            kv_grad,
            *arrived,
            logit_grad,
            projected,
            cosine,
            sine,
            head_gain,
        )
        in_grads.append(in_grad)
        key_gain_sums.append(key_terms[0])
    query_gain, key_gain_sum = query_gain[0] + query_gain[1], key_gain_sums[0] + key_gain_sums[1]
    head_gains = jnp.stack([query_gain, key_gain_sum])
    head_gains = head_gains + swap_core(head_gains)
    head_gains = head_gains + swap_x(head_gains)
    first, second, head_gains = settle(gate_up_back, *in_grads, head_gains)
    in_back = Scatter(
        lambda slot, right=jnp.concatenate((first, second)), middle_low=jnp.concatenate(
            middle_lows
        ): jnp.concatenate(
            [
                transpose_by(normed_one[:, slot * depth : (slot + 1) * depth], right),
                transpose_by(middle_low[:, slot * depth : (slot + 1) * depth], gated_all),
            ],
            axis=1,
        ),
        count,
    )
    first, second = in_back.issue(first, second)
    first = by_transpose(first, in_full).astype(bf16)
    second = by_transpose(second, in_full).astype(bf16)
    chips = [chip_sum(partial[own_rows:], partial[:own_rows]) for partial in (first, second)]
    from_x = [swap_x(chip) for chip in chips]
    chips[1], head_gains = pump(in_back, chips[1], head_gains)
    drain(gate_up_back)
    drain(down_back)
    gate_up_grad = gate_up_back.total()
    down_grad = down_back.total()
    mlp_sum = jnp.sum(
        gate_up_grad[:, :hidden_units] * gate_weight.astype(f32)
        + gate_up_grad[:, hidden_units:] * up_weight.astype(f32),
        axis=1,
    )
    gate_grad, up_grad = gate_up_grad[:, :hidden_units], gate_up_grad[:, hidden_units:]
    level, turn = 1, 0
    while level < count // 2:
        if turn == 1:
            from_x[1], gate_grad, up_grad, down_grad, mlp_sum = order(
                from_x[1], gate_grad, up_grad, down_grad, mlp_sum
            )
        late = min(turn, MICRO_BATCHES - 1)
        arrived_gains, from_x[late] = pump(in_back, swap_dp(head_gains, level), from_x[late])
        head_gains = head_gains + arrived_gains
        level, turn = 2 * level, turn + 1
    input_rows = []
    for micro in range(MICRO_BATCHES):
        part = pl.BlockSpec((own_rows // 2, width), lambda i: (i, 0))
        input_rows.append(
            pl.pallas_call(
                input_back_kernel,
                out_shape=jax.ShapeDtypeStruct((own_rows, width), f32),
                grid=(2,),
                in_specs=[
                    pl.BlockSpec(
                        (own_rows // 2, width), lambda i, micro=micro: (4 * micro + i, 0)
                    ),
                    part,
                    part,
                    whole(1, width),
                    part,
                ],
                out_specs=part,
                compiler_params=params,
                cost_estimate=cost(1024, 1024),
                name="input_back",
            )(inputs_low, chips[micro], from_x[micro], gain_attn, middle_grads[micro])
        )
    other_rows = [swap_core(rows) for rows in input_rows]
    if depth % 128:
        tokens_grad = place_back(jnp.stack(input_rows), jnp.stack(other_rows), True, "place_tokens")
    else:
        tokens_grad = pl.pallas_call(
            place_rows_kernel,
            out_shape=jax.ShapeDtypeStruct((MICRO_BATCHES, 2, own_rows, width), f32),
            grid_spec=pltpu.PrefetchScalarGridSpec(
                num_scalar_prefetch=2,
                grid=(count,),
                in_specs=[pl.BlockSpec((own_rows, depth), lambda i, cols, core: (0, i))]
                * (2 * MICRO_BATCHES),
                out_specs=pl.BlockSpec(
                    (MICRO_BATCHES, 2, own_rows, depth), lambda i, cols, core: (0, 0, 0, cols[i])
                ),
            ),
            compiler_params=params,
            cost_estimate=cost(1024, 1024),
            name="place_tokens",
        )(column_places, core_place, *input_rows, *other_rows).reshape(total_rows, width)

    arrived_gains, tokens_grad = pump(in_back, swap_dp(head_gains, level), tokens_grad)
    head_gains = head_gains + arrived_gains
    tokens_grad = drain(in_back, tokens_grad)
    in_total = in_back.total()
    in_weight_grad, out_weight_grad = in_total[:, :joined], in_total[:, joined:].T
    used = first_gain
    attn_sum = jnp.sum(in_weight_grad[:, :used] * packed[:, :used].astype(f32), axis=1)
    gains = jnp.stack([attn_sum, mlp_sum])
    for swap in (swap_core, swap_x):
        gains = gains + swap(gains)
    return (
        layer_out,
        tokens_grad,
        in_weight_grad[:, :query_cols],
        in_weight_grad[:, query_cols : query_cols + key_cols],
        in_weight_grad[:, query_cols + key_cols : query_cols + 2 * key_cols],
        in_weight_grad[:, query_cols + 2 * key_cols : query_cols + 2 * key_cols + head_count],
        out_weight_grad,
        gate_grad,
        up_grad,
        down_grad,
        gains[0] / norm_attn.astype(f32),
        gains[1] / norm_mlp.astype(f32),
        head_gains[0],
        head_gains[1],
    )


def solution(mesh):
    rows, weight, turned = P("dp", None), P("dp", "mp"), P("mp", "dp")
    weights = (weight, weight, weight, weight, turned, weight, weight, turned)
    placed = (rows, rows) + weights + (P("dp"), P("dp"), P(), P())
    return jax.shard_map(
        on_device, mesh=mesh, in_specs=placed + (P(),), out_specs=placed, check_vma=False
    )
```
